32 devices in a mesh: frames: 8 (over z, x), heads: 4 (over y, core).
Axes of the slice: x: 2, y: 2, z: 4, core: 2. Of those that a mesh axis runs over, the one named last changes fastest.
Arguments:
- frames: bfloat16 [8192, 1024], P('frames', 'heads'), may hold values from -6 to 6
- latents: bfloat16 [512, 1024], replicated, may hold values from -6 to 6
- cross_query: bfloat16 [2, 1024, 1024], P(None, None, 'heads'), may hold values from -0.1875 to 0.1875
- cross_key: bfloat16 [2, 1024, 1024], P(None, None, 'heads'), may hold values from -0.1875 to 0.1875
- cross_value: bfloat16 [2, 1024, 1024], P(None, None, 'heads'), may hold values from -0.1875 to 0.1875
- cross_out: bfloat16 [2, 1024, 1024], P(None, 'heads'), may hold values from -0.1875 to 0.1875
- self_query: bfloat16 [2, 1024, 1024], P(None, None, 'heads'), may hold values from -0.1875 to 0.1875
- self_key: bfloat16 [2, 1024, 1024], P(None, None, 'heads'), may hold values from -0.1875 to 0.1875
- self_value: bfloat16 [2, 1024, 1024], P(None, None, 'heads'), may hold values from -0.1875 to 0.1875
- self_out: bfloat16 [2, 1024, 1024], P(None, 'heads'), may hold values from -0.1875 to 0.1875
- mlp_in: bfloat16 [2, 1024, 4096], P(None, None, 'heads'), may hold values from -0.1875 to 0.1875
- mlp_out: bfloat16 [2, 4096, 1024], P(None, 'heads'), may hold values from -0.09375 to 0.09375
Outputs:
- encoded: float32 [512, 1024], P('frames')
- midway: float32 [512, 1024], P(None, 'heads')
The draws below stay inside these ranges and needn't reach their ends.
All inputs are finite; a program needn't handle non-finite values.
Results may differ from the reference program's by a relative error of at most 0.007.
Values may be sent and summed in bfloat16 or wider, within the bound.
No kernel may reach another device: no remote copies, remote signals or barrier semaphores. Data moves between devices by JAX's collectives and lax.ppermute only.
A program may use at most 64 MiB of HBM per device.

```python
import math
import jax
import jax.numpy as jnp
from jax import lax

D = 1024
HEADS = 16
HEAD_DIM = 64
LATENTS = 512
FF = 4096
PASSES = 2
FRAMES = 8192


def base_weight(key, seed_offset):
    random_part = jax.random.truncated_normal(jax.random.fold_in(key, seed_offset), -6.0, 6.0, (PASSES, D, D), jnp.float32)
    return random_part / math.sqrt(D)


def drawn_query(key, seed_offset):
    values = base_weight(key, seed_offset)
    return values.astype(jnp.bfloat16)


def drawn_key(key, seed_offset):
    values = base_weight(key, seed_offset)
    return values.astype(jnp.bfloat16)


def draw_cross_query(key, part):
    return drawn_query(key, 101)


def draw_cross_key(key, part):
    return drawn_key(key, 102)


def draw_self_query(key, part):
    return drawn_query(key, 103)


def draw_self_key(key, part):
    return drawn_key(key, 104)


def draw_frames(key, part):
    random_part = jax.random.truncated_normal(jax.random.fold_in(key, 31), -6.0, 6.0, (FRAMES, D), jnp.float32)
    return random_part.astype(jnp.bfloat16)


def draw_latents(key, part):
    random_part = jax.random.truncated_normal(jax.random.fold_in(key, 41), -6.0, 6.0, (LATENTS, D), jnp.float32)
    return random_part.astype(jnp.bfloat16)


def level_of(key, extent, cuts, least, top_value):
    level, own = 1.0, jax.random.fold_in(key, 6)
    for position, shards_of in cuts:
        steps = jnp.exp(jax.random.uniform(jax.random.fold_in(own, position), (shards_of,), jnp.float32, least / len(cuts), top_value / len(cuts)))
        level = level * jnp.repeat(steps, extent[position] // shards_of).reshape([-1 if axis == position else 1 for axis in range(len(extent))])
    return level


def centred(stream_key, shape, deviation, bound, shards=(), kind=jnp.bfloat16):
    entries = deviation * jax.random.normal(stream_key, shape, jnp.float32)
    if shards:
        entries = entries * level_of(stream_key, shape, shards, -0.22, 0.18)
    return jnp.clip(entries, -bound, bound).astype(kind)


def setup_inputs(seed: int = 0) -> dict:
    key_of = jax.random.split(jax.random.key(seed), 13)
    return {
        "frames": draw_frames(jax.random.fold_in(key_of[12], 71), 0),
        "latents": draw_latents(jax.random.fold_in(key_of[12], 71), 0),
        "cross_query": draw_cross_query(jax.random.fold_in(key_of[12], 71), 0),
        "cross_key": draw_cross_key(jax.random.fold_in(key_of[12], 71), 0),
        "cross_value": centred(key_of[4], (PASSES, D, D), D ** -0.5, 0.1875, ((2, 4),)),
        "cross_out": centred(key_of[5], (PASSES, D, D), D ** -0.5, 0.1875, ((1, 4),)),
        "self_query": draw_self_query(jax.random.fold_in(key_of[12], 71), 0),
        "self_key": draw_self_key(jax.random.fold_in(key_of[12], 71), 0),
        "self_value": centred(key_of[8], (PASSES, D, D), D ** -0.5, 0.1875, ((2, 4),)),
        "self_out": centred(key_of[9], (PASSES, D, D), D ** -0.5, 0.1875, ((1, 4),)),
        "mlp_in": centred(key_of[10], (PASSES, D, FF), D ** -0.5, 0.1875, ((2, 4),)),
        "mlp_out": centred(key_of[11], (PASSES, FF, D), FF ** -0.5, 0.09375, ((1, 4),)),
    }


epsilon = 1e-05

def layer_norm(vector):
    centre = vector - lax.optimization_barrier(jnp.mean(vector, axis=-1, keepdims=True))
    spread_sq = lax.optimization_barrier(jnp.mean(centre * centre, axis=-1, keepdims=True))
    return centre * lax.rsqrt(spread_sq + epsilon)

def project(left_side, weight):
    return jnp.dot(left_side, weight, preferred_element_type=jnp.float32)

def cross_context(queries, key_rows, value_rows):
    latent_count = queries.shape[0]
    frame_count = key_rows.shape[0]
    query_heads = queries.reshape(latent_count, HEADS, HEAD_DIM).transpose(1, 0, 2)
    key_heads = key_rows.reshape(frame_count, HEADS, HEAD_DIM).transpose(1, 0, 2)
    value_heads = value_rows.reshape(frame_count, HEADS, HEAD_DIM).transpose(1, 0, 2)

    def one_head(triple):
        query_one, key_one, value_one = triple
        scores = jnp.dot(query_one, key_one.T, preferred_element_type=jnp.float32)
        highest = lax.optimization_barrier(jnp.max(scores, axis=1, keepdims=True))
        exponent_terms = jnp.exp(scores - highest)
        totals = lax.optimization_barrier(jnp.sum(exponent_terms, axis=1, keepdims=True))
        weighted = jnp.dot(exponent_terms, value_one.astype(jnp.float32), precision=lax.Precision.HIGHEST)
        return (weighted / totals).astype(jnp.bfloat16)
    outcome = lax.map(one_head, (query_heads, key_heads, value_heads))
    return outcome.transpose(1, 0, 2).reshape(latent_count, HEADS * HEAD_DIM)

def self_context(queries, key_rows, value_rows):
    latent_count = queries.shape[0]
    query_heads = queries.reshape(latent_count, HEADS, HEAD_DIM).astype(jnp.float32)
    key_heads = key_rows.reshape(latent_count, HEADS, HEAD_DIM).astype(jnp.float32)
    value_heads = value_rows.reshape(latent_count, HEADS, HEAD_DIM).astype(jnp.float32)
    scores = jnp.einsum('ihd,khd->hik', query_heads, key_heads)
    weights = jax.nn.softmax(scores, axis=-1).astype(jnp.bfloat16)
    context = jnp.einsum('hik,khd->ihd', weights.astype(jnp.float32), value_heads)
    return context.reshape(latent_count, HEADS * HEAD_DIM).astype(jnp.bfloat16)

def reference(frames, latents, cross_query, cross_key, cross_value, cross_out, self_query, self_key, self_value, self_out, mlp_in, mlp_out):
    score_scale = 1.0 / HEAD_DIM ** 0.5
    normed = layer_norm(frames.astype(jnp.float32)).astype(jnp.bfloat16)
    latent_state = latents.astype(jnp.float32)
    midway = latent_state
    for pass_index in range(PASSES):
        cross_in = layer_norm(latent_state).astype(jnp.bfloat16)
        queries = (project(cross_in, cross_query[pass_index]) * score_scale).astype(jnp.bfloat16)
        key_rows = project(normed, cross_key[pass_index]).astype(jnp.bfloat16)
        value_rows = project(normed, cross_value[pass_index]).astype(jnp.bfloat16)
        context = cross_context(queries, key_rows, value_rows)
        latent_state = latent_state + project(context, cross_out[pass_index])
        self_in = layer_norm(latent_state).astype(jnp.bfloat16)
        self_q = (project(self_in, self_query[pass_index]) * score_scale).astype(jnp.bfloat16)
        self_k = project(self_in, self_key[pass_index]).astype(jnp.bfloat16)
        self_v = project(self_in, self_value[pass_index]).astype(jnp.bfloat16)
        context = self_context(self_q, self_k, self_v)
        latent_state = latent_state + project(context, self_out[pass_index])
        mlp_norm = layer_norm(latent_state).astype(jnp.bfloat16)
        hidden = jax.nn.gelu(project(mlp_norm, mlp_in[pass_index]), approximate=False).astype(jnp.bfloat16)
        latent_state = latent_state + project(hidden, mlp_out[pass_index])
        if pass_index == 0:
            midway = latent_state
    return (latent_state, midway)
```

```python
import jax
import jax.numpy as jnp
from jax import lax
from jax.sharding import PartitionSpec as P

HEAD_DIM = 64
epsilon = 1e-05


def shifted(value, axis, step):
    count = lax.axis_size(axis)
    return lax.ppermute(value, axis, [(i, (i + step) % count) for i in range(count)])


WIDEST = 8


def origin(axis, k):
    if lax.axis_size(axis) > WIDEST:
        return k
    return (lax.axis_index(axis) - k) % lax.axis_size(axis)


def gathered_blocks(value, axis):
    count = lax.axis_size(axis)
    if count > WIDEST:
        pieces = lax.all_gather(value, axis)
        return [pieces[k] for k in range(count)]
    return [value] + [shifted(value, axis, k) for k in range(1, count)]


def returned_blocks(blocks, axis):
    count = lax.axis_size(axis)
    if count > WIDEST:
        pieces = lax.all_to_all(jnp.stack(blocks), axis, 0, 0, tiled=True)
        return [pieces[k] for k in range(count)]
    return [blocks[0]] + [shifted(blocks[k], axis, -k) for k in range(1, count)]


def layer_norm(vector):
    centre = vector - jnp.mean(vector, axis=-1, keepdims=True)
    spread_sq = jnp.mean(centre * centre, axis=-1, keepdims=True)
    return centre * lax.rsqrt(spread_sq + epsilon)


def project(left_side, weight):
    return jnp.dot(left_side, weight, preferred_element_type=jnp.float32)


def placed_blocks(blocks, axis_name, dim):
    count = lax.axis_size(axis_name)
    size = blocks[0].shape[dim]
    if count > WIDEST:
        return jnp.concatenate(blocks, dim)
    shape = list(blocks[0].shape)
    shape[dim] = size * count
    total = jnp.zeros(shape, blocks[0].dtype)
    for k, block in enumerate(blocks):
        total = lax.dynamic_update_slice_in_dim(total, block, origin(axis_name, k) * size, dim)
    return total


def partial_cross(queries, key_rows, value_rows):
    rows, columns = queries.shape
    heads = columns // HEAD_DIM
    query_heads = queries.reshape(rows, heads, HEAD_DIM)
    key_heads = key_rows.reshape(-1, heads, HEAD_DIM)
    value_heads = value_rows.reshape(-1, heads, HEAD_DIM)
    scores = jnp.einsum("lhd,fhd->hlf", query_heads, key_heads, preferred_element_type=jnp.float32)
    highest = jnp.max(scores, axis=2)
    terms = jnp.exp(scores - highest[:, :, None])
    totals = jnp.sum(terms, axis=2)
    weighted = jnp.einsum(
        "hlf,fhd->lhd", terms.astype(jnp.bfloat16), value_heads, preferred_element_type=jnp.float32
    )
    return weighted.reshape(rows, columns).astype(jnp.bfloat16), highest.T, totals.T


def merged_cross(weighted, highest, totals):
    weighted = jnp.stack(weighted).astype(jnp.float32)
    highest = jnp.stack(highest)
    totals = jnp.stack(totals)
    top = jnp.max(highest, axis=0)
    factor = jnp.exp(highest - top)
    total = jnp.sum(factor * totals, axis=0)
    share = jnp.repeat(factor / total, HEAD_DIM, axis=2)
    return jnp.sum(weighted * share, axis=0).astype(jnp.bfloat16)


def self_context(queries, key_rows, value_rows):
    rows, columns = queries.shape
    heads = columns // HEAD_DIM
    query_heads = queries.reshape(rows, heads, HEAD_DIM)
    key_heads = key_rows.reshape(-1, heads, HEAD_DIM)
    value_heads = value_rows.reshape(-1, heads, HEAD_DIM)
    scores = jnp.einsum("ihd,khd->hik", query_heads, key_heads, preferred_element_type=jnp.float32)
    weights = jax.nn.softmax(scores, axis=-1).astype(jnp.bfloat16)
    context = jnp.einsum("hik,khd->ihd", weights, value_heads, preferred_element_type=jnp.float32)
    return context.reshape(rows, columns).astype(jnp.bfloat16)


def local(
    frames,
    latents,
    cross_query,
    cross_key,
    cross_value,
    cross_out,
    self_query,
    self_key,
    self_value,
    self_out,
    mlp_in,
    mlp_out,
):
    score_scale = 1.0 / HEAD_DIM**0.5
    passes = cross_query.shape[0]
    shards, me = lax.axis_size("frames"), lax.axis_index("frames")
    row_count = latents.shape[0] // shards
    columns = cross_query.shape[2]
    gathered = placed_blocks(gathered_blocks(frames, "heads"), "heads", 1)
    normed = layer_norm(gathered.astype(jnp.float32)).astype(jnp.bfloat16)
    blocks = [
        lax.dynamic_slice_in_dim(latents, origin("frames", k) * row_count, row_count, 0)
        for k in range(shards)
    ]
    state = lax.dynamic_slice_in_dim(latents, me * row_count, row_count, 0).astype(jnp.float32)
    all_rows = jnp.concatenate(blocks, 0).astype(jnp.float32)
    queries = (project(layer_norm(all_rows).astype(jnp.bfloat16), cross_query[0]) * score_scale).astype(
        jnp.bfloat16
    )
    cross_weights = [None] * passes
    self_weights = [None] * passes
    for p in range(passes):
        cross_weights[p] = placed_blocks(gathered_blocks(cross_out[p], "heads"), "heads", 0)
        self_weights[p] = placed_blocks(gathered_blocks(self_out[p], "heads"), "heads", 0)
    for p in range(passes):
        key_rows = project(normed, cross_key[p]).astype(jnp.bfloat16)
        value_rows = project(normed, cross_value[p]).astype(jnp.bfloat16)
        weighted, highest, totals = partial_cross(queries, key_rows, value_rows)
        stats = jnp.concatenate([highest, totals], 1)
        parts = [
            (
                weighted[k * row_count : (k + 1) * row_count],
                stats[k * row_count : (k + 1) * row_count],
            )
            for k in range(shards)
        ]
        weighted = returned_blocks([part[0] for part in parts], "frames")
        stats = returned_blocks([part[1] for part in parts], "frames")
        heads = columns // HEAD_DIM
        context = merged_cross(weighted, [s[:, :heads] for s in stats], [s[:, heads:] for s in stats])
        context = lax.all_gather(context, "heads", axis=1, tiled=True)
        state = state + project(context, cross_weights[p])
        self_in = layer_norm(state).astype(jnp.bfloat16)
        self_q = (project(self_in, self_query[p]) * score_scale).astype(jnp.bfloat16)
        self_k = project(self_in, self_key[p]).astype(jnp.bfloat16)
        self_v = project(self_in, self_value[p]).astype(jnp.bfloat16)
        both = gathered_blocks(jnp.concatenate([self_k, self_v], 1), "frames")
        both = jnp.concatenate(both, 0)
        context = self_context(self_q, both[:, :columns], both[:, columns:])
        context = lax.all_gather(context, "heads", axis=1, tiled=True)
        state = state + project(context, self_weights[p])
        mlp_norm = layer_norm(state).astype(jnp.bfloat16)
        hidden = jax.nn.gelu(project(mlp_norm, mlp_in[p]), approximate=False).astype(jnp.bfloat16)
        partial = project(hidden, mlp_out[p]).astype(jnp.bfloat16)
        partial = lax.all_gather(partial, "heads")
        state = state + jnp.sum(partial.astype(jnp.float32), axis=0)
        if p == 0:
            own = lax.dynamic_slice_in_dim(state, lax.axis_index("heads") * columns, columns, 1)
            midway = placed_blocks(gathered_blocks(own, "frames"), "frames", 0)
        if p + 1 < passes:
            cross_in = layer_norm(state).astype(jnp.bfloat16)
            own = (project(cross_in, cross_query[p + 1]) * score_scale).astype(jnp.bfloat16)
            queries = jnp.concatenate(gathered_blocks(own, "frames"), 0)
    return (state, midway)


def solution(mesh):
    columns, rows = P(None, None, "heads"), P(None, "heads", None)
    placed = (P("frames", "heads"), P(), columns, columns, columns, rows)
    placed = placed + (columns, columns, columns, rows, columns, rows)
    return jax.shard_map(
        local,
        mesh=mesh,
        in_specs=placed,
        out_specs=(P("frames", None), P(None, "heads")),
        check_vma=False,
    )
```

```python
import functools

import jax
import jax.numpy as jnp
from jax import lax
from jax.experimental import pallas as pl
from jax.experimental.pallas import tpu as pltpu
from jax.sharding import PartitionSpec as P

HEAD_DIM = 64
STATS = 4
WIDEST = 8
epsilon = 1e-05
f32, bf16 = jnp.float32, jnp.bfloat16


def shifted(value, axis, step):
    count = lax.axis_size(axis)
    return lax.ppermute(value, axis, [(i, (i + step) % count) for i in range(count)])


def gathered_blocks(value, axis):
    count = lax.axis_size(axis)
    if count > WIDEST:
        pieces = lax.all_gather(value, axis)
        return [pieces[k] for k in range(count)]
    return [value] + [shifted(value, axis, k) for k in range(1, count)]


def feature_blocks(value):
    count, me = lax.axis_size("heads"), lax.axis_index("heads")
    own, owner = [value], [me]
    for k in range(2, count, 2):
        own.append(shifted(value, "heads", k))
        owner.append((me - k) % count)
    swap = [(i, i ^ 1) for i in range(count)]
    other = [lax.ppermute(block, "heads", swap) for block in own]
    partner = me ^ 1
    others = [(partner - k) % count for k in range(0, count, 2)]
    return own + other, owner + others


def whole_call(body, results, *operands):
    space = pl.BlockSpec(memory_space=pltpu.VMEM)
    return pl.pallas_call(
        body,
        out_shape=results,
        in_specs=[space] * len(operands),
        out_specs=jax.tree.map(lambda _: space, results),
    )(*operands)


def shaped(shape, dtype):
    return jax.ShapeDtypeStruct(shape, dtype)


def normed(vector):
    centre = vector - jnp.mean(vector, axis=-1, keepdims=True)
    spread_sq = jnp.mean(centre * centre, axis=-1, keepdims=True)
    return (centre * lax.rsqrt(spread_sq + epsilon)).astype(bf16)


def product(left_side, weight):
    return jnp.dot(left_side, weight, preferred_element_type=f32)


def contracted(left_side, right_side, left_dim, right_dim, precision=None):
    return lax.dot_general(
        left_side,
        right_side,
        (((left_dim,), (right_dim,)), ((), ())),
        precision=precision,
        preferred_element_type=f32,
    )


def frames_kernel(owner_ref, *refs):
    count = owner_ref.shape[0]
    blocks, (key_w, value_w), outs = refs[:count], refs[count : count + 2], refs[count + 2 :]
    passes, width = key_w.shape[0], blocks[0].shape[1]
    pieces = [block[...].astype(f32) for block in blocks]
    total = sum(jnp.sum(piece, axis=1, keepdims=True) for piece in pieces)
    mean = total / (width * count)
    pieces = [piece - mean for piece in pieces]
    total = sum(jnp.sum(piece * piece, axis=1, keepdims=True) for piece in pieces)
    scale = lax.rsqrt(total / (width * count) + epsilon)
    pieces = [(piece * scale).astype(bf16) for piece in pieces]
    starts = [pl.multiple_of(owner_ref[j] * width, width) for j in range(count)]
    for p in range(passes):
        for weight, out, turned in ((key_w, outs[2 * p], False), (value_w, outs[2 * p + 1], True)):
            made = sum(
                product(pieces[j], weight[p, pl.ds(starts[j], width), :]) for j in range(count)
            )
            out[...] = (made.T if turned else made).astype(bf16)


def frames_call(blocks, owners, key_weights, value_weights):
    count, rows, width = len(blocks), *blocks[0].shape
    passes, depth, columns = key_weights.shape
    tile = min(rows, 256)
    weights = pl.BlockSpec((passes, depth, columns), lambda i, o: (0, 0, 0))
    results = [shaped((rows, columns), bf16), shaped((columns, rows), bf16)] * passes
    placed = [
        pl.BlockSpec((tile, columns), lambda i, o: (i, 0)),
        pl.BlockSpec((columns, tile), lambda i, o: (0, i)),
    ] * passes
    return pl.pallas_call(
        frames_kernel,
        out_shape=results,
        grid_spec=pltpu.PrefetchScalarGridSpec(
            num_scalar_prefetch=1,
            grid=(rows // tile,),
            in_specs=[pl.BlockSpec((tile, width), lambda i, o: (i, 0))] * count + [weights] * 2,
            out_specs=placed,
        ),
    )(jnp.stack(owners).astype(jnp.int32), *blocks, key_weights, value_weights)


def split_terms(value):
    high = value.astype(bf16).astype(f32)
    return high, (value - high).astype(bf16).astype(f32)


def partial_kernel(queries, keys, values, out):
    latents, columns = queries.shape
    shards, rows = out.shape[0], latents // out.shape[0]
    heads = columns // HEAD_DIM
    chunk = min(latents, 256)
    lane_head = lax.broadcasted_iota(jnp.int32, (chunk, columns), 1) // HEAD_DIM
    all_keys = keys[...]
    for start in range(0, latents, chunk):
        some = queries[start : start + chunk, :]
        pieces, tops, tops_low, sums, sums_low = [], [], [], [], []
        for h in range(heads):
            one = jnp.where(lane_head == h, some, jnp.zeros_like(some))
            scores = contracted(all_keys, one, 1, 1)
            high, low = split_terms(jnp.max(scores, axis=0, keepdims=True))
            terms = jnp.exp(scores - (high + low))
            tops.append(high)
            tops_low.append(low)
            high, low = split_terms(jnp.sum(terms, axis=0, keepdims=True))
            sums.append(high)
            sums_low.append(low)
            pieces.append(product(values[h * HEAD_DIM : (h + 1) * HEAD_DIM, :], terms.astype(bf16)))
        turned = jnp.concatenate(pieces, axis=0).T.astype(bf16)
        stats = tops + tops_low + sums + sums_low
        spare = out.shape[1] - rows - len(stats)
        stats = stats + [jnp.zeros((1, chunk), f32)] * spare
        stats = jnp.concatenate(stats, axis=0)
        for j in range(chunk // rows):
            block = start // rows + j
            out[block, :rows, :] = turned[j * rows : (j + 1) * rows, :]
            piece = stats[:, j * rows : (j + 1) * rows]
            piece = jnp.concatenate(
                [piece, jnp.zeros((piece.shape[0], columns - rows), f32)], axis=1
            )
            out[block, rows:, :] = piece.astype(bf16)


def merge_kernel(parts, weight, out):
    shards, columns = parts.shape[0], parts.shape[2]
    heads = columns // HEAD_DIM
    rows = out.shape[0]
    tops, sums = [], []
    for s in range(shards):
        stats = parts[s, rows:, :].astype(f32)[:, :rows]
        tops.append(stats[0:heads] + stats[heads : 2 * heads])
        sums.append(stats[2 * heads : 3 * heads] + stats[3 * heads : 4 * heads])
    highest = functools.reduce(jnp.maximum, tops)
    factors = [jnp.exp(top - highest) for top in tops]
    total = sum(factor * one for factor, one in zip(factors, sums))
    factors = jnp.concatenate([factor / total for factor in factors], axis=0)
    shape = (shards * heads, shards * columns)
    row = lax.broadcasted_iota(jnp.int32, shape, 0)
    lane = lax.broadcasted_iota(jnp.int32, shape, 1)
    spreader = (lane // HEAD_DIM == row).astype(f32)
    factors = contracted(factors, spreader, 0, 0, lax.Precision.HIGHEST)
    context = jnp.zeros((rows, columns), f32)
    for s in range(shards):
        context += factors[:, s * columns : (s + 1) * columns] * parts[s, :rows, :].astype(f32)
    out[...] = product(context.astype(bf16), weight[...]).astype(bf16)


def updated(state, parts):
    return state[...] + sum(parts[h].astype(f32) for h in range(parts.shape[0]))


def project_kernel(scale, state, parts, query_w, key_w, value_w, new_state, query, both):
    value = updated(state, parts)
    new_state[...] = value
    value = normed(value)
    columns = query_w.shape[1]
    query[...] = (product(value, query_w[...]) * scale).astype(bf16)
    both[:, :columns] = product(value, key_w[...]).astype(bf16)
    both[:, columns:] = product(value, value_w[...]).astype(bf16)


def attend_kernel(query, *refs):
    blocks, weight, out = refs[:-2], refs[-2], refs[-1]
    rows, columns = query.shape
    both = jnp.concatenate([block[...] for block in blocks], axis=0)
    keys, values = both[:, :columns], both[:, columns:]
    lane_head = lax.broadcasted_iota(jnp.int32, (rows, columns), 1) // HEAD_DIM
    context = jnp.zeros((rows, columns), f32)
    for h in range(columns // HEAD_DIM):
        one = jnp.where(lane_head == h, query[...], jnp.zeros((rows, columns), bf16))
        scores = contracted(one, keys, 1, 1)
        terms = jnp.exp(scores - jnp.max(scores, axis=1, keepdims=True))
        share = (terms / jnp.sum(terms, axis=1, keepdims=True)).astype(bf16)
        context = jnp.where(lane_head == h, product(share, values), context)
    out[...] = product(context.astype(bf16), weight[...]).astype(bf16)


def mlp_kernel(state, parts, in_w, out_w, new_state, out):
    value = updated(state, parts)
    new_state[...] = value
    hidden = product(normed(value), in_w[...])
    hidden = 0.5 * hidden * (1.0 + lax.erf(hidden * 0.5**0.5))
    out[...] = product(hidden.astype(bf16), out_w[...]).astype(bf16)


def query_kernel(scale, state, parts, query_w, new_state, query):
    value = updated(state, parts)
    new_state[...] = value
    made = (product(normed(value), query_w[...]) * scale).astype(bf16)
    for k in range(query.shape[0]):
        query[k] = made


def final_kernel(state, parts, new_state):
    new_state[...] = updated(state, parts)


def local(
    frames,
    latents,
    cross_query,
    cross_key,
    cross_value,
    cross_out,
    self_query,
    self_key,
    self_value,
    self_out,
    mlp_in,
    mlp_out,
):
    scale = 1.0 / HEAD_DIM**0.5
    passes, width, columns = cross_query.shape
    shards, me = lax.axis_size("frames"), lax.axis_index("frames")
    latent_count = latents.shape[0]
    rows = latent_count // shards
    stat_rows = -(-STATS * (columns // HEAD_DIM) // 16) * 16
    projections = frames_call(*feature_blocks(frames), cross_key, cross_value)
    state = lax.dynamic_slice_in_dim(latents, me * rows, rows, 0).astype(f32)
    queries = (product(normed(latents.astype(f32)), cross_query[0]) * scale).astype(bf16)
    state_shape = shaped((rows, width), f32)
    part_shape = shaped((rows, width), bf16)
    row_shape = shaped((rows, columns), bf16)
    for p in range(passes):
        parts = whole_call(
            partial_kernel,
            shaped((shards, rows + stat_rows, columns), bf16),
            queries,
            projections[2 * p],
            projections[2 * p + 1],
        )
        parts = lax.all_to_all(parts, "frames", 0, 0)
        part = whole_call(merge_kernel, part_shape, parts, cross_out[p])
        state, query, both = whole_call(
            functools.partial(project_kernel, scale),
            (state_shape, row_shape, shaped((rows, 2 * columns), bf16)),
            state,
            lax.all_gather(part, "heads"),
            self_query[p],
            self_key[p],
            self_value[p],
        )
        blocks = gathered_blocks(both, "frames")
        part = whole_call(attend_kernel, part_shape, query, *blocks, self_out[p])
        state, part = whole_call(
            mlp_kernel,
            (state_shape, part_shape),
            state,
            lax.all_gather(part, "heads"),
            mlp_in[p],
            mlp_out[p],
        )
        part = lax.all_gather(part, "heads")
        if p + 1 < passes:
            state, queries = whole_call(
                functools.partial(query_kernel, scale),
                (state_shape, shaped((shards, rows, columns), bf16)),
                state,
                part,
                cross_query[p + 1],
            )
            queries = lax.all_to_all(queries, "frames", 0, 0).reshape(latent_count, columns)
        else:
            state = whole_call(final_kernel, state_shape, state, part)
        if p == 0:
            own = lax.dynamic_slice_in_dim(state, lax.axis_index("heads") * columns, columns, 1)
            own = jnp.broadcast_to(own[None], (shards, rows, columns))
            midway = lax.all_to_all(own, "frames", 0, 0).reshape(latent_count, columns)
    return (state, midway)


def solution(mesh):
    columns, rows = P(None, None, "heads"), P(None, "heads", None)
    placed = (P("frames", "heads"), P(), columns, columns, columns, rows)
    placed = placed + (columns, columns, columns, rows, columns, rows)
    return jax.shard_map(
        local,
        mesh=mesh,
        in_specs=placed,
        out_specs=(P("frames", None), P(None, "heads")),
        check_vma=False,
    )
```

```python
import functools

import jax
import jax.numpy as jnp
from jax import lax
from jax.experimental import pallas as pl
from jax.experimental.pallas import tpu as pltpu
from jax.sharding import PartitionSpec as P

HEAD_DIM = 64
STATS = 4
VMEM_BYTES = 20 << 20
WIDEST = 8
epsilon = 1e-05
f32, bf16 = jnp.float32, jnp.bfloat16


def shifted(value, axis, step):
    count = lax.axis_size(axis)
    return lax.ppermute(value, axis, [(i, (i + step) % count) for i in range(count)])


def gathered_blocks(value, axis):
    count = lax.axis_size(axis)
    if count > WIDEST:
        pieces = lax.all_gather(value, axis)
        return [pieces[k] for k in range(count)]
    return [value] + [shifted(value, axis, k) for k in range(1, count)]


def line_of(count):
    return [list(range(x, count, 2)) for x in range(2)]


def line_shift(value, step):
    count = lax.axis_size("frames")
    return lax.ppermute(value, "frames", [(i, (i + 2 * step) % count) for i in range(count)])


def line_gather(value):
    count = lax.axis_size("frames")
    if count > WIDEST:
        pieces = lax.all_gather(value, "frames", axis_index_groups=line_of(count))
        return [pieces[k] for k in range(count // 2)]
    return [value] + [line_shift(value, k) for k in range(1, count // 2)]


def line_return(blocks):
    count = lax.axis_size("frames")
    if count > WIDEST:
        groups = line_of(count)
        pieces = lax.all_to_all(jnp.stack(blocks), "frames", 0, 0, axis_index_groups=groups)
        return [pieces[k] for k in range(count // 2)]
    return [blocks[0]] + [line_shift(blocks[k], -k) for k in range(1, count // 2)]


def pair_swap(value):
    count = lax.axis_size("frames")
    return lax.ppermute(value, "frames", [(i, i ^ 1) for i in range(count)])


def feature_blocks(value):
    count, me = lax.axis_size("heads"), lax.axis_index("heads")
    own, owner = [value], [me]
    for k in range(2, count, 2):
        own.append(shifted(value, "heads", k))
        owner.append((me - k) % count)
    swap = [(i, i ^ 1) for i in range(count)]
    other = [lax.ppermute(block, "heads", swap) for block in own]
    partner = me ^ 1
    others = [(partner - k) % count for k in range(0, count, 2)]
    return own + other, owner + others


def whole_call(body, results, *operands, cost=None):
    space = pl.BlockSpec(memory_space=pltpu.VMEM)
    return pl.pallas_call(
        body,
        out_shape=results,
        in_specs=[space] * len(operands),
        out_specs=jax.tree.map(lambda _: space, results),
        compiler_params=pltpu.CompilerParams(vmem_limit_bytes=VMEM_BYTES),
        cost_estimate=cost,
    )(*operands)


def shaped(shape, dtype):
    return jax.ShapeDtypeStruct(shape, dtype)


def normed(vector):
    centre = vector - jnp.mean(vector, axis=-1, keepdims=True)
    spread_sq = jnp.mean(centre * centre, axis=-1, keepdims=True)
    return (centre * lax.rsqrt(spread_sq + epsilon)).astype(bf16)


def product(left_side, weight):
    return jnp.dot(left_side, weight, preferred_element_type=f32)


def contracted(left_side, right_side, left_dim, right_dim, precision=None):
    return lax.dot_general(
        left_side,
        right_side,
        (((left_dim,), (right_dim,)), ((), ())),
        precision=precision,
        preferred_element_type=f32,
    )


def place(index):
    return jnp.asarray(index, jnp.int32).reshape(1, 1)


def norm_kernel(*refs):
    out = refs[-1]
    count = (len(refs) - 1) // 2
    blocks, owners = refs[:count], refs[count:-1]
    rows, width = blocks[0].shape
    tile = min(rows, 256)
    for start in range(0, rows, tile):
        pieces = [block[start : start + tile, :].astype(f32) for block in blocks]
        total = sum(jnp.sum(piece, axis=1, keepdims=True) for piece in pieces)
        mean = total / (width * count)
        pieces = [piece - mean for piece in pieces]
        total = sum(jnp.sum(piece * piece, axis=1, keepdims=True) for piece in pieces)
        scale = lax.rsqrt(total / (width * count) + epsilon)
        for piece, owner in zip(pieces, owners):
            lanes = pl.ds(pl.multiple_of(owner[0, 0] * width, width), width)
            out[start : start + tile, lanes] = (piece * scale).astype(bf16)


def frames_call(blocks, owners):
    rows, width = blocks[0].shape
    space = pl.BlockSpec(memory_space=pltpu.VMEM)
    scalar = pl.BlockSpec(memory_space=pltpu.SMEM)
    return pl.pallas_call(
        norm_kernel,
        out_shape=shaped((rows, width * len(blocks)), bf16),
        in_specs=[space] * len(blocks) + [scalar] * len(owners),
        out_specs=space,
        compiler_params=pltpu.CompilerParams(vmem_limit_bytes=VMEM_BYTES),
    )(*blocks, *[place(owner) for owner in owners])


def key_value_kernel(p, rows, key_w, value_w, keys, values):
    keys[...] = product(rows[...], key_w[p]).astype(bf16)
    values[...] = product(rows[...], value_w[p]).astype(bf16).T


def split_terms(value):
    high = value.astype(bf16).astype(f32)
    return high, (value - high).astype(bf16).astype(f32)


def partial_kernel(query_count, key_count, rows, *refs):
    query_refs, refs = refs[:query_count], refs[query_count:]
    key_refs, refs = refs[:key_count], refs[key_count:]
    value_refs, outs = refs[:key_count], refs[key_count:]
    if query_count > 1:
        queries = jnp.concatenate([ref[...] for ref in query_refs], axis=0)
    else:
        queries = query_refs[0][...]
    if len(outs) == 1:
        outs = [outs[0].at[k] for k in range(outs[0].shape[0])]
    latents, columns = queries.shape
    heads = columns // HEAD_DIM
    chunk = min(latents, 256)
    lane_head = lax.broadcasted_iota(jnp.int32, (chunk, columns), 1) // HEAD_DIM
    for start in range(0, latents, chunk):
        some = queries[start : start + chunk, :]
        pieces, tops, tops_low, sums, sums_low = [], [], [], [], []
        for h in range(heads):
            one = jnp.where(lane_head == h, some, jnp.zeros_like(some))
            scores = [contracted(keys[...], one, 1, 1) for keys in key_refs]
            top = functools.reduce(
                jnp.maximum, [jnp.max(part, axis=0, keepdims=True) for part in scores]
            )
            high, low = split_terms(top)
            terms = [jnp.exp(part - (high + low)) for part in scores]
            tops.append(high)
            tops_low.append(low)
            high, low = split_terms(sum(jnp.sum(part, axis=0, keepdims=True) for part in terms))
            sums.append(high)
            sums_low.append(low)
            lanes = slice(h * HEAD_DIM, (h + 1) * HEAD_DIM)
            pieces.append(
                sum(product(v[lanes, :], part.astype(bf16)) for v, part in zip(value_refs, terms))
            )
        turned = jnp.concatenate(pieces, axis=0).T.astype(bf16)
        stats = tops + tops_low + sums + sums_low
        spare = outs[0].shape[0] - rows - len(stats)
        stats = stats + [jnp.zeros((1, chunk), f32)] * spare
        stats = jnp.concatenate(stats, axis=0)
        for j in range(chunk // rows):
            out = outs[start // rows + j]
            out[:rows, :] = turned[j * rows : (j + 1) * rows, :]
            piece = stats[:, j * rows : (j + 1) * rows]
            piece = jnp.concatenate(
                [piece, jnp.zeros((piece.shape[0], columns - rows), f32)], axis=1
            )
            out[rows:, :] = piece.astype(bf16)


def merge_kernel(p, *refs):
    parts, weight, out = refs[:-2], refs[-2], refs[-1]
    if len(parts) == 1:
        parts = [parts[0].at[k] for k in range(parts[0].shape[0])]
    shards, columns = len(parts), parts[0].shape[1]
    heads = columns // HEAD_DIM
    rows = out.shape[0]
    tops, sums = [], []
    for s in range(shards):
        stats = parts[s][rows:, :].astype(f32)[:, :rows]
        tops.append(stats[0:heads] + stats[heads : 2 * heads])
        sums.append(stats[2 * heads : 3 * heads] + stats[3 * heads : 4 * heads])
    highest = functools.reduce(jnp.maximum, tops)
    factors = [jnp.exp(top - highest) for top in tops]
    total = sum(factor * one for factor, one in zip(factors, sums))
    factors = jnp.concatenate([factor / total for factor in factors], axis=0)
    shape = (shards * heads, shards * columns)
    row = lax.broadcasted_iota(jnp.int32, shape, 0)
    lane = lax.broadcasted_iota(jnp.int32, shape, 1)
    spreader = (lane // HEAD_DIM == row).astype(f32)
    factors = contracted(factors, spreader, 0, 0, lax.Precision.HIGHEST)
    context = jnp.zeros((rows, columns), f32)
    for s in range(shards):
        context += factors[:, s * columns : (s + 1) * columns] * parts[s][:rows, :].astype(f32)
    out[...] = product(context.astype(bf16), weight[p]).astype(bf16)


def updated(state, parts):
    return state[...] + sum(parts[h].astype(f32) for h in range(parts.shape[0]))


def project_kernel(p, scale, state, parts, query_w, key_w, value_w, new_state, query, both):
    value = updated(state, parts)
    new_state[...] = value
    value = normed(value)
    columns = query_w.shape[2]
    query[...] = (product(value, query_w[p]) * scale).astype(bf16)
    both[:, :columns] = product(value, key_w[p]).astype(bf16)
    both[:, columns:] = product(value, value_w[p]).astype(bf16)


def attend_kernel(p, query, *refs):
    blocks, weight, out = refs[:-2], refs[-2], refs[-1]
    rows, columns = query.shape
    both = jnp.concatenate([block[...] for block in blocks], axis=0)
    keys, values = both[:, :columns], both[:, columns:]
    lane_head = lax.broadcasted_iota(jnp.int32, (rows, columns), 1) // HEAD_DIM
    context = jnp.zeros((rows, columns), f32)
    for h in range(columns // HEAD_DIM):
        one = jnp.where(lane_head == h, query[...], jnp.zeros((rows, columns), bf16))
        scores = contracted(one, keys, 1, 1)
        terms = jnp.exp(scores - jnp.max(scores, axis=1, keepdims=True))
        share = (terms / jnp.sum(terms, axis=1, keepdims=True)).astype(bf16)
        context = jnp.where(lane_head == h, product(share, values), context)
    out[...] = product(context.astype(bf16), weight[p]).astype(bf16)


def mlp_kernel(p, state, parts, in_w, out_w, new_state, out):
    value = updated(state, parts)
    new_state[...] = value
    hidden = product(normed(value), in_w[p])
    hidden = 0.5 * hidden * (1.0 + lax.erf(hidden * 0.5**0.5))
    out[...] = product(hidden.astype(bf16), out_w[p]).astype(bf16)


def query_kernel(p, scale, state, parts, index, query_w, new_state, query, share):
    value = updated(state, parts)
    new_state[...] = value
    query[...] = (product(normed(value), query_w[p]) * scale).astype(bf16)
    columns = share.shape[2]
    own = new_state[:, pl.ds(pl.multiple_of(index[0, 0] * columns, columns), columns)]
    for k in range(share.shape[0]):
        share[k] = own


def final_kernel(state, parts, new_state):
    new_state[...] = updated(state, parts)


def local(
    frames,
    latents,
    cross_query,
    cross_key,
    cross_value,
    cross_out,
    self_query,
    self_key,
    self_value,
    self_out,
    mlp_in,
    mlp_out,
):
    scale = 1.0 / HEAD_DIM**0.5
    passes, width, columns = cross_query.shape
    shards, me = lax.axis_size("frames"), lax.axis_index("frames")
    latent_count = latents.shape[0]
    rows = latent_count // shards
    stat_rows = -(-STATS * (columns // HEAD_DIM) // 16) * 16
    rows_normed = frames_call(*feature_blocks(frames))
    depth, frame_count = rows_normed.shape[1], rows_normed.shape[0]
    state = lax.dynamic_slice_in_dim(latents, me * rows, rows, 0).astype(f32)
    queries = [(product(normed(latents.astype(f32)), cross_query[0]) * scale).astype(bf16)]
    state_shape = shaped((rows, width), f32)
    part_shape = shaped((rows, width), bf16)
    row_shape = shaped((rows, columns), bf16)
    packed_shape = shaped((rows + stat_rows, columns), bf16)
    key_values = [
        whole_call(
            functools.partial(key_value_kernel, p),
            (shaped((frame_count, columns), bf16), shaped((columns, frame_count), bf16)),
            rows_normed,
            cross_key,
            cross_value,
            cost=pl.CostEstimate(
                flops=4 * frame_count * depth * columns,
                bytes_accessed=2 * frame_count * depth,
                transcendentals=0,
            ),
        )
        for p in range(passes)
    ]
    for p in range(passes):
        keys, values = [key_values[p][0]], [key_values[p][1]]
        if p == 0:
            packed = shaped((shards,) + packed_shape.shape, bf16)
        else:
            keys, values = keys + [pair_swap(keys[0])], values + [pair_swap(values[0])]
            packed = [packed_shape] * len(queries)
        parts = whole_call(
            functools.partial(partial_kernel, len(queries), len(keys), rows),
            packed,
            *queries,
            *keys,
            *values,
        )
        parts = [lax.all_to_all(parts, "frames", 0, 0)] if p == 0 else line_return(parts)
        part = whole_call(functools.partial(merge_kernel, p), part_shape, *parts, cross_out)
        state, query, both = whole_call(
            functools.partial(project_kernel, p, scale),
            (state_shape, row_shape, shaped((rows, 2 * columns), bf16)),
            state,
            lax.all_gather(part, "heads"),
            self_query,
            self_key,
            self_value,
        )
        blocks = gathered_blocks(both, "frames")
        part = whole_call(functools.partial(attend_kernel, p), part_shape, query, *blocks, self_out)
        state, part = whole_call(
            functools.partial(mlp_kernel, p),
            (state_shape, part_shape),
            state,
            lax.all_gather(part, "heads"),
            mlp_in,
            mlp_out,
        )
        part = lax.all_gather(part, "heads")
        if p + 1 == passes:
            state = whole_call(final_kernel, state_shape, state, part)
            break
        space = pl.BlockSpec(memory_space=pltpu.VMEM)
        state, query, share = pl.pallas_call(
            functools.partial(query_kernel, p + 1, scale),
            out_shape=(state_shape, row_shape, shaped((shards, rows, columns), f32)),
            in_specs=[space, space, pl.BlockSpec(memory_space=pltpu.SMEM), space],
            out_specs=(space,) * 3,
            compiler_params=pltpu.CompilerParams(vmem_limit_bytes=VMEM_BYTES),
        )(state, part, place(lax.axis_index("heads")), cross_query)
        queries = line_gather(query)
        if p == 0:
            midway = lax.all_to_all(share, "frames", 0, 0).reshape(latent_count, columns)
    return (state, midway)


def solution(mesh):
    columns, rows = P(None, None, "heads"), P(None, "heads", None)
    placed = (P("frames", "heads"), P(), columns, columns, columns, rows)
    placed = placed + (columns, columns, columns, rows, columns, rows)
    return jax.shard_map(
        local,
        mesh=mesh,
        in_specs=placed,
        out_specs=(P("frames", None), P(None, "heads")),
        check_vma=False,
    )
```

```python
import functools

import jax
import jax.numpy as jnp
from jax import lax
from jax.experimental import pallas as pl
from jax.experimental.pallas import tpu as pltpu
from jax.sharding import PartitionSpec as P

HEAD_DIM = 64
STATS = 4
VMEM_BYTES = 20 << 20
WIDEST = 8
epsilon = 1e-05
f32, bf16 = jnp.float32, jnp.bfloat16


def shifted(value, axis, step):
    count = lax.axis_size(axis)
    return lax.ppermute(value, axis, [(i, (i + step) % count) for i in range(count)])


def origin(count, widest, k, me):
    return k if count > widest else lax.rem(me - k + count, count)


def gathered_blocks(value, axis):
    count = lax.axis_size(axis)
    if count > WIDEST:
        pieces = lax.all_gather(value, axis)
        return [pieces[k] for k in range(count)]
    return [value] + [shifted(value, axis, k) for k in range(1, count)]


def returned_blocks(blocks, axis):
    count = lax.axis_size(axis)
    if count > WIDEST:
        pieces = lax.all_to_all(jnp.stack(blocks), axis, 0, 0)
        return [pieces[k] for k in range(count)]
    return [blocks[0]] + [shifted(blocks[k], axis, -k) for k in range(1, count)]


def line_of(count):
    return [list(range(x, count, 2)) for x in range(2)]


def line_shift(value, step):
    count = lax.axis_size("frames")
    return lax.ppermute(value, "frames", [(i, (i + 2 * step) % count) for i in range(count)])


def line_gather(value):
    count = lax.axis_size("frames")
    if count > WIDEST:
        pieces = lax.all_gather(value, "frames", axis_index_groups=line_of(count))
        return [pieces[k] for k in range(count // 2)]
    return [value] + [line_shift(value, k) for k in range(1, count // 2)]


def line_return(blocks):
    count = lax.axis_size("frames")
    if count > WIDEST:
        groups = line_of(count)
        pieces = lax.all_to_all(jnp.stack(blocks), "frames", 0, 0, axis_index_groups=groups)
        return [pieces[k] for k in range(count // 2)]
    return [blocks[0]] + [line_shift(blocks[k], -k) for k in range(1, count // 2)]


def pair_swap(value):
    count = lax.axis_size("frames")
    return lax.ppermute(value, "frames", [(i, i ^ 1) for i in range(count)])


def feature_blocks(value, alongside):
    count, me = lax.axis_size("heads"), lax.axis_index("heads")
    own, owner = [value], [me]
    for k in range(2, count, 2):
        own.append(shifted(value, "heads", k))
        owner.append((me - k) % count)
    swap = [(i, i ^ 1) for i in range(count)]
    own[1:], alongside = lax.optimization_barrier((own[1:], alongside))
    other = [lax.ppermute(block, "heads", swap) for block in own]
    partner = me ^ 1
    others = [(partner - k) % count for k in range(0, count, 2)]
    return own + other, owner + others, alongside


def whole_call(body, results, *operands, cost=None, scalars=(), scratch=()):
    space = pl.BlockSpec(memory_space=pltpu.VMEM)
    scalar = pl.BlockSpec(memory_space=pltpu.SMEM)
    return pl.pallas_call(
        body,
        out_shape=results,
        in_specs=[space] * len(operands) + [scalar] * len(scalars),
        out_specs=jax.tree.map(lambda _: space, results),
        scratch_shapes=scratch,
        compiler_params=pltpu.CompilerParams(vmem_limit_bytes=VMEM_BYTES),
        cost_estimate=cost,
    )(*operands, *[jnp.asarray(index, jnp.int32).reshape(1, 1) for index in scalars])


def shaped(shape, dtype):
    return jax.ShapeDtypeStruct(shape, dtype)


def normed(vector):
    centre = vector - jnp.mean(vector, axis=-1, keepdims=True)
    spread_sq = jnp.mean(centre * centre, axis=-1, keepdims=True)
    return (centre * lax.rsqrt(spread_sq + epsilon)).astype(bf16)


def product(left_side, weight):
    return jnp.dot(left_side, weight, preferred_element_type=f32)


def contracted(left_side, right_side, left_dim, right_dim, precision=None):
    return lax.dot_general(
        left_side,
        right_side,
        (((left_dim,), (right_dim,)), ((), ())),
        precision=precision,
        preferred_element_type=f32,
    )


def norm_kernel(*refs):
    out = refs[-1]
    count = (len(refs) - 1) // 2
    blocks, owners = refs[:count], refs[count:-1]
    rows, width = blocks[0].shape
    tile = min(rows, 256)
    for start in range(0, rows, tile):
        pieces = [block[start : start + tile, :].astype(f32) for block in blocks]
        total = sum(jnp.sum(piece, axis=1, keepdims=True) for piece in pieces)
        mean = total / (width * count)
        pieces = [piece - mean for piece in pieces]
        total = sum(jnp.sum(piece * piece, axis=1, keepdims=True) for piece in pieces)
        scale = lax.rsqrt(total / (width * count) + epsilon)
        for piece, owner in zip(pieces, owners):
            lanes = pl.ds(pl.multiple_of(owner[0, 0] * width, width), width)
            out[start : start + tile, lanes] = (piece * scale).astype(bf16)


def key_value_kernel(p, rows, key_w, value_w, keys, values):
    keys[...] = product(rows[...], key_w[p]).astype(bf16)
    values[...] = product(rows[...], value_w[p]).astype(bf16).T


def latents_kernel(scale, count, latents, query_w, me, state, queries, rows_normed):
    rows = state.shape[0]
    for k in range(count):
        start = origin(count, WIDEST, k, me[0, 0]) * rows
        value = latents[pl.ds(pl.multiple_of(start, rows), rows), :].astype(f32)
        rows_normed[k * rows : (k + 1) * rows, :] = normed(value)
    state[...] = latents[pl.ds(pl.multiple_of(me[0, 0] * rows, rows), rows), :].astype(f32)
    queries[...] = (product(rows_normed[...], query_w[0]) * scale).astype(bf16)


def split_terms(value):
    high = value.astype(bf16).astype(f32)
    return high, (value - high).astype(bf16).astype(f32)


def partial_kernel(query_count, key_count, rows, *refs):
    query_refs, refs = refs[:query_count], refs[query_count:]
    key_refs, refs = refs[:key_count], refs[key_count:]
    value_refs, outs = refs[:key_count], refs[key_count:]
    columns = key_refs[0].shape[1]
    if query_count > 1:
        queries = jnp.concatenate([ref[:, :columns] for ref in query_refs], axis=0)
        for k, ref in enumerate(query_refs):
            outs[-1][k * rows : (k + 1) * rows, :] = ref[:, columns:]
        outs = outs[:-1]
    else:
        queries = query_refs[0][...]
    latents = queries.shape[0]
    heads = columns // HEAD_DIM
    chunk = min(latents, 256)
    lane_head = lax.broadcasted_iota(jnp.int32, (chunk, columns), 1) // HEAD_DIM
    for start in range(0, latents, chunk):
        some = queries[start : start + chunk, :]
        pieces, tops, tops_low, sums, sums_low = [], [], [], [], []
        for h in range(heads):
            one = jnp.where(lane_head == h, some, jnp.zeros_like(some))
            scores = [contracted(keys[...], one, 1, 1) for keys in key_refs]
            top = functools.reduce(
                jnp.maximum, [jnp.max(part, axis=0, keepdims=True) for part in scores]
            )
            high, low = split_terms(top)
            terms = [jnp.exp(part - (high + low)) for part in scores]
            tops.append(high)
            tops_low.append(low)
            high, low = split_terms(sum(jnp.sum(part, axis=0, keepdims=True) for part in terms))
            sums.append(high)
            sums_low.append(low)
            lanes = slice(h * HEAD_DIM, (h + 1) * HEAD_DIM)
            pieces.append(
                sum(product(v[lanes, :], part.astype(bf16)) for v, part in zip(value_refs, terms))
            )
        turned = jnp.concatenate(pieces, axis=0).T.astype(bf16)
        stats = tops + tops_low + sums + sums_low
        spare = outs[0].shape[0] - rows - len(stats)
        stats = stats + [jnp.zeros((1, chunk), f32)] * spare
        stats = jnp.concatenate(stats, axis=0)
        for j in range(chunk // rows):
            out = outs[start // rows + j]
            out[:rows, :] = turned[j * rows : (j + 1) * rows, :]
            piece = stats[:, j * rows : (j + 1) * rows]
            piece = jnp.concatenate(
                [piece, jnp.zeros((piece.shape[0], columns - rows), f32)], axis=1
            )
            out[rows:, :] = piece.astype(bf16)


def merge_kernel(p, *refs):
    parts, weight, out = refs[:-2], refs[-2], refs[-1]
    shards, columns = len(parts), parts[0].shape[1]
    heads = columns // HEAD_DIM
    rows = out.shape[0]
    tops, sums = [], []
    for s in range(shards):
        stats = parts[s][rows:, :].astype(f32)[:, :rows]
        tops.append(stats[0:heads] + stats[heads : 2 * heads])
        sums.append(stats[2 * heads : 3 * heads] + stats[3 * heads : 4 * heads])
    highest = functools.reduce(jnp.maximum, tops)
    factors = [jnp.exp(top - highest) for top in tops]
    total = sum(factor * one for factor, one in zip(factors, sums))
    factors = jnp.concatenate([factor / total for factor in factors], axis=0)
    shape = (shards * heads, shards * columns)
    row = lax.broadcasted_iota(jnp.int32, shape, 0)
    lane = lax.broadcasted_iota(jnp.int32, shape, 1)
    spreader = (lane // HEAD_DIM == row).astype(f32)
    factors = contracted(factors, spreader, 0, 0, lax.Precision.HIGHEST)
    context = jnp.zeros((rows, columns), f32)
    for s in range(shards):
        context += factors[:, s * columns : (s + 1) * columns] * parts[s][:rows, :].astype(f32)
    out[...] = product(context.astype(bf16), weight[p]).astype(bf16)


def updated(state, parts):
    return state[...] + sum(parts[h].astype(f32) for h in range(parts.shape[0]))


def project_kernel(p, scale, state, parts, query_w, key_w, value_w, new_state, query, both):
    value = updated(state, parts)
    new_state[...] = value
    value = normed(value)
    columns = query_w.shape[2]
    query[...] = (product(value, query_w[p]) * scale).astype(bf16)
    both[:, :columns] = product(value, key_w[p]).astype(bf16)
    both[:, columns:] = product(value, value_w[p]).astype(bf16)


def attend_kernel(p, query, *refs):
    blocks, weight, out = refs[:-2], refs[-2], refs[-1]
    rows, columns = query.shape
    both = jnp.concatenate([block[...] for block in blocks], axis=0)
    keys, values = both[:, :columns], both[:, columns:]
    lane_head = lax.broadcasted_iota(jnp.int32, (rows, columns), 1) // HEAD_DIM
    context = jnp.zeros((rows, columns), f32)
    for h in range(columns // HEAD_DIM):
        one = jnp.where(lane_head == h, query[...], jnp.zeros((rows, columns), bf16))
        scores = contracted(one, keys, 1, 1)
        terms = jnp.exp(scores - jnp.max(scores, axis=1, keepdims=True))
        share = (terms / jnp.sum(terms, axis=1, keepdims=True)).astype(bf16)
        context = jnp.where(lane_head == h, product(share, values), context)
    out[...] = product(context.astype(bf16), weight[p]).astype(bf16)


def mlp_kernel(p, state, parts, in_w, out_w, new_state, out):
    value = updated(state, parts)
    new_state[...] = value
    hidden = product(normed(value), in_w[p])
    hidden = 0.5 * hidden * (1.0 + lax.erf(hidden * 0.5**0.5))
    out[...] = product(hidden.astype(bf16), out_w[p]).astype(bf16)


def query_kernel(p, scale, state, parts, query_w, index, new_state, message):
    value = updated(state, parts)
    new_state[...] = value
    columns = query_w.shape[2]
    message[:, :columns] = (product(normed(value), query_w[p]) * scale).astype(bf16)
    own = new_state[:, pl.ds(pl.multiple_of(index[0, 0] * columns, columns), columns)]
    message[:, columns:] = own.astype(bf16)


def final_kernel(count, state, parts, share, other_share, me, new_state, midway):
    new_state[...] = updated(state, parts)
    rows = new_state.shape[0]
    line, side = me[0, 0] // 2, lax.rem(me[0, 0], 2)
    for k in range(count // 2):
        place_of = 2 * origin(count // 2, WIDEST // 2, k, line)
        for block, at in ((share, place_of + side), (other_share, place_of + 1 - side)):
            start = pl.multiple_of(at * rows, rows)
            midway[pl.ds(start, rows), :] = block[k * rows : (k + 1) * rows, :].astype(f32)


def local(
    frames,
    latents,
    cross_query,
    cross_key,
    cross_value,
    cross_out,
    self_query,
    self_key,
    self_value,
    self_out,
    mlp_in,
    mlp_out,
):
    scale = 1.0 / HEAD_DIM**0.5
    passes, width, columns = cross_query.shape
    shards, me = lax.axis_size("frames"), lax.axis_index("frames")
    latent_count = latents.shape[0]
    rows = latent_count // shards
    stat_rows = -(-STATS * (columns // HEAD_DIM) // 16) * 16
    state_shape = shaped((rows, width), f32)
    part_shape = shaped((rows, width), bf16)
    row_shape = shaped((rows, columns), bf16)
    double_shape = shaped((rows, 2 * columns), bf16)
    packed_shape = shaped((rows + stat_rows, columns), bf16)
    state, queries = whole_call(
        functools.partial(latents_kernel, scale, shards),
        (state_shape, shaped((latent_count, columns), bf16)),
        latents,
        cross_query,
        scalars=(me,),
        scratch=[pltpu.VMEM((latent_count, width), bf16)],
        cost=pl.CostEstimate(
            flops=2 * latent_count * width * columns,
            bytes_accessed=2 * latent_count * width,
            transcendentals=0,
        ),
    )
    blocks, owners, queries = feature_blocks(frames, queries)
    queries = [queries]
    frame_count = frames.shape[0]
    rows_normed = whole_call(
        norm_kernel, shaped((frame_count, width), bf16), *blocks, scalars=owners
    )
    key_values = [
        whole_call(
            functools.partial(key_value_kernel, p),
            (shaped((frame_count, columns), bf16), shaped((columns, frame_count), bf16)),
            rows_normed,
            cross_key,
            cross_value,
            cost=pl.CostEstimate(
                flops=4 * frame_count * width * columns,
                bytes_accessed=2 * frame_count * width,
                transcendentals=0,
            ),
        )
        for p in range(passes)
    ]
    for p in range(passes):
        keys, values = [key_values[p][0]], [key_values[p][1]]
        if p > 0:
            keys, values = keys + [pair_swap(keys[0])], values + [pair_swap(values[0])]
        call = functools.partial(partial_kernel, len(queries), len(keys), rows)
        if p == 0:
            parts = whole_call(call, [packed_shape] * shards, *queries, *keys, *values)
            parts = returned_blocks(parts, "frames")
        else:
            results = [packed_shape] * len(queries) + [shaped((rows * len(queries), columns), bf16)]
            *parts, share = whole_call(call, results, *queries, *keys, *values)
            parts = line_return(parts)
            if p == 1:
                first_share = share
        part = whole_call(functools.partial(merge_kernel, p), part_shape, *parts, cross_out)
        state, query, both = whole_call(
            functools.partial(project_kernel, p, scale),
            (state_shape, row_shape, double_shape),
            state,
            lax.all_gather(part, "heads"),
            self_query,
            self_key,
            self_value,
        )
        blocks = gathered_blocks(both, "frames")
        part = whole_call(functools.partial(attend_kernel, p), part_shape, query, *blocks, self_out)
        state, part = whole_call(
            functools.partial(mlp_kernel, p),
            (state_shape, part_shape),
            state,
            lax.all_gather(part, "heads"),
            mlp_in,
            mlp_out,
        )
        part = lax.all_gather(part, "heads")
        if p + 1 < passes:
            state, message = whole_call(
                functools.partial(query_kernel, p + 1, scale),
                (state_shape, double_shape),
                state,
                part,
                cross_query,
                scalars=(lax.axis_index("heads"),),
            )
            queries = line_gather(message)
        else:
            state, midway = whole_call(
                functools.partial(final_kernel, shards),
                (state_shape, shaped((latent_count, columns), f32)),
                state,
                part,
                first_share,
                pair_swap(first_share),
                scalars=(me,),
            )
    return (state, midway)


def solution(mesh):
    columns, rows = P(None, None, "heads"), P(None, "heads", None)
    placed = (P("frames", "heads"), P(), columns, columns, columns, rows)
    placed = placed + (columns, columns, columns, rows, columns, rows)
    return jax.shard_map(
        local,
        mesh=mesh,
        in_specs=placed,
        out_specs=(P("frames", None), P(None, "heads")),
        check_vma=False,
    )
```

```python
import functools

import jax
import jax.numpy as jnp
from jax import lax
from jax.experimental import pallas as pl
from jax.experimental.pallas import tpu as pltpu
from jax.sharding import PartitionSpec as P

HEAD_DIM = 64
STATS = 4
VMEM_BYTES = 10 << 20
CHUNKS = 2
WIDEST = 8
epsilon = 1e-05
f32, bf16 = jnp.float32, jnp.bfloat16


def shifted(value, axis, step):
    count = lax.axis_size(axis)
    return lax.ppermute(value, axis, [(i, (i + step) % count) for i in range(count)])


def origin(count, widest, k, me):
    return k if count > widest else lax.rem(me - k + count, count)


def gathered_blocks(value, axis):
    count = lax.axis_size(axis)
    if count > WIDEST:
        pieces = lax.all_gather(value, axis)
        return [pieces[k] for k in range(count)]
    return [value] + [shifted(value, axis, k) for k in range(1, count)]


def returned_blocks(blocks, axis):
    count = lax.axis_size(axis)
    if count > WIDEST:
        pieces = lax.all_to_all(jnp.stack(blocks), axis, 0, 0)
        return [pieces[k] for k in range(count)]
    return [blocks[0]] + [shifted(blocks[k], axis, -k) for k in range(1, count)]


def line_of(count):
    return [list(range(x, count, 2)) for x in range(2)]


def line_shift(value, step):
    count = lax.axis_size("frames")
    return lax.ppermute(value, "frames", [(i, (i + 2 * step) % count) for i in range(count)])


def line_gather(value):
    count = lax.axis_size("frames")
    if count > WIDEST:
        pieces = lax.all_gather(value, "frames", axis_index_groups=line_of(count))
        return [pieces[k] for k in range(count // 2)]
    return [value] + [line_shift(value, k) for k in range(1, count // 2)]


def line_return(blocks):
    count = lax.axis_size("frames")
    if count > WIDEST:
        groups = line_of(count)
        pieces = lax.all_to_all(jnp.stack(blocks), "frames", 0, 0, axis_index_groups=groups)
        return [pieces[k] for k in range(count // 2)]
    return [blocks[0]] + [line_shift(blocks[k], -k) for k in range(1, count // 2)]


def pair_swap(value):
    count = lax.axis_size("frames")
    return lax.ppermute(value, "frames", [(i, i ^ 1) for i in range(count)])


def pass_on(blocks, alongside):
    count = lax.axis_size("heads")
    blocks, alongside = lax.optimization_barrier((blocks, alongside))
    swap = [(i, i ^ 1) for i in range(count)]
    return blocks + [lax.ppermute(block, "heads", swap) for block in blocks], alongside


def whole_call(body, results, *operands, cost=None, scalars=(), scratch=()):
    space = pl.BlockSpec(memory_space=pltpu.VMEM)
    scalar = pl.BlockSpec(memory_space=pltpu.SMEM)
    return pl.pallas_call(
        body,
        out_shape=results,
        in_specs=[space] * len(operands) + [scalar] * len(scalars),
        out_specs=jax.tree.map(lambda _: space, results),
        scratch_shapes=scratch,
        compiler_params=pltpu.CompilerParams(vmem_limit_bytes=VMEM_BYTES),
        cost_estimate=cost,
    )(*operands, *[jnp.asarray(index, jnp.int32).reshape(1, 1) for index in scalars])


def shaped(shape, dtype):
    return jax.ShapeDtypeStruct(shape, dtype)


def normed(vector):
    centre = vector - jnp.mean(vector, axis=-1, keepdims=True)
    spread_sq = jnp.mean(centre * centre, axis=-1, keepdims=True)
    return (centre * lax.rsqrt(spread_sq + epsilon)).astype(bf16)


def product(left_side, weight):
    return jnp.dot(left_side, weight, preferred_element_type=f32)


def contracted(left_side, right_side, left_dim, right_dim, precision=None):
    return lax.dot_general(
        left_side,
        right_side,
        (((left_dim,), (right_dim,)), ((), ())),
        precision=precision,
        preferred_element_type=f32,
    )


def frames_kernel(chunk, *refs):
    (key_w, value_w), (out, keys, values) = refs[:2], refs[-3:]
    refs = refs[2:-3]
    count = len(refs) // 2
    blocks, owners = refs[:count], refs[count:]
    rows, width = out.shape[0], blocks[0].shape[1]
    tile = min(rows, 32)
    for start in range(0, rows, tile):
        pieces = []
        for block in blocks:
            first = start + (chunk * rows if block.shape[0] > rows else 0)
            pieces.append(block[first : first + tile, :].astype(f32))
        mean = jnp.sum(sum(pieces), axis=1, keepdims=True) / (width * count)
        pieces = [piece - mean for piece in pieces]
        total = jnp.sum(sum(piece * piece for piece in pieces), axis=1, keepdims=True)
        scale = lax.rsqrt(total / (width * count) + epsilon)
        for piece, owner in zip(pieces, owners):
            lanes = pl.ds(pl.multiple_of(owner[0, 0] * width, width), width)
            out[start : start + tile, lanes] = (piece * scale).astype(bf16)
    key_value_kernel(0, out, key_w, value_w, keys, values)


def key_value_kernel(p, *refs):
    row_refs, (key_w, value_w, keys, values) = refs[:-4], refs[-4:]
    start = 0
    for rows in row_refs:
        end = start + rows.shape[0]
        keys[start:end, :] = product(rows[...], key_w[p]).astype(bf16)
        values[:, start:end] = product(rows[...], value_w[p]).astype(bf16).T
        start = end


def latents_kernel(scale, count, latents, query_w, me, state, queries, rows_normed):
    rows = state.shape[0]
    for k in range(count):
        start = origin(count, WIDEST, k, me[0, 0]) * rows
        value = latents[pl.ds(pl.multiple_of(start, rows), rows), :].astype(f32)
        rows_normed[k * rows : (k + 1) * rows, :] = normed(value)
    state[...] = latents[pl.ds(pl.multiple_of(me[0, 0] * rows, rows), rows), :].astype(f32)
    queries[...] = (product(rows_normed[...], query_w[0]) * scale).astype(bf16)


def split_terms(value):
    high = value.astype(bf16).astype(f32)
    return high, (value - high).astype(bf16).astype(f32)


def partial_kernel(query_count, key_count, rows, carried, last, *refs):
    query_refs, refs = refs[:query_count], refs[query_count:]
    key_refs, refs = refs[:key_count], refs[key_count:]
    value_refs, refs = refs[:key_count], refs[key_count:]
    carry, outs = (refs[:2], refs[2:]) if carried else (None, refs)
    columns = key_refs[0].shape[1]
    if query_count > 1:
        queries = jnp.concatenate([ref[:, :columns] for ref in query_refs], axis=0)
        for k, ref in enumerate(query_refs):
            outs[-1][k * rows : (k + 1) * rows, :] = ref[:, columns:]
        outs = outs[:-1]
    else:
        queries = query_refs[0][...]
    latents = queries.shape[0]
    heads = columns // HEAD_DIM
    chunk = min(latents, 256)
    span = min(columns, 128)
    lane_head = lax.broadcasted_iota(jnp.int32, (chunk, span), 1) // HEAD_DIM

    def scores_of(start, h):
        lanes = slice(h * HEAD_DIM // span * span, (h * HEAD_DIM // span + 1) * span)
        some = queries[start : start + chunk, lanes]
        mine = lane_head == h % (span // HEAD_DIM)
        one = jnp.where(mine, some, jnp.zeros_like(some))
        return [contracted(keys[:, lanes], one, 1, 1) for keys in key_refs]

    order = [(start, h) for start in range(0, latents, chunk) for h in range(heads)]
    coming = scores_of(*order[0])
    for start in range(0, latents, chunk):
        pieces, tops, sums = [], [], []
        for h in range(heads):
            scores, following = coming, order.index((start, h)) + 1
            if following < len(order):
                coming = scores_of(*order[following])
            top = functools.reduce(
                jnp.maximum, [jnp.max(part, axis=0, keepdims=True) for part in scores]
            )
            own = slice(h * HEAD_DIM, (h + 1) * HEAD_DIM)
            if carried:
                before = carry[1][h : h + 1, start : start + chunk]
                top = jnp.maximum(top, before)
            high, low = split_terms(top)
            top = high + low
            terms = [jnp.exp(part - top) for part in scores]
            total = sum(jnp.sum(part, axis=0, keepdims=True) for part in terms)
            piece = sum(product(v[own, :], part.astype(bf16)) for v, part in zip(value_refs, terms))
            if carried:
                factor = jnp.exp(before - top)
                total += factor * carry[1][heads + h : heads + h + 1, start : start + chunk]
                piece += factor * carry[0][own, start : start + chunk]
            if last:
                tops.append((high, low))
                sums.append(split_terms(total))
                pieces.append(piece)
            else:
                outs[0][own, start : start + chunk] = piece
                outs[1][h : h + 1, start : start + chunk] = top
                outs[1][heads + h : heads + h + 1, start : start + chunk] = total
        if not last:
            continue
        turned = jnp.concatenate(pieces, axis=0).T.astype(bf16)
        stats = [pair[0] for pair in tops] + [pair[1] for pair in tops]
        stats += [pair[0] for pair in sums] + [pair[1] for pair in sums]
        spare = outs[0].shape[0] - rows - len(stats)
        stats = stats + [jnp.zeros((1, chunk), f32)] * spare
        stats = jnp.concatenate(stats, axis=0)
        for j in range(chunk // rows):
            out = outs[start // rows + j]
            out[:rows, :] = turned[j * rows : (j + 1) * rows, :]
            piece = stats[:, j * rows : (j + 1) * rows]
            piece = jnp.concatenate(
                [piece, jnp.zeros((piece.shape[0], columns - rows), f32)], axis=1
            )
            out[rows:, :] = piece.astype(bf16)


def merge_kernel(p, *refs):
    parts, weight, out = refs[:-2], refs[-2], refs[-1]
    shards, columns = len(parts), parts[0].shape[1]
    heads = columns // HEAD_DIM
    rows = out.shape[0]
    tops, sums = [], []
    for s in range(shards):
        stats = parts[s][rows:, :].astype(f32)[:, :rows]
        tops.append(stats[0:heads] + stats[heads : 2 * heads])
        sums.append(stats[2 * heads : 3 * heads] + stats[3 * heads : 4 * heads])
    highest = functools.reduce(jnp.maximum, tops)
    factors = [jnp.exp(top - highest) for top in tops]
    total = sum(factor * one for factor, one in zip(factors, sums))
    factors = jnp.concatenate([factor / total for factor in factors], axis=0)
    shape = (shards * heads, shards * columns)
    row = lax.broadcasted_iota(jnp.int32, shape, 0)
    lane = lax.broadcasted_iota(jnp.int32, shape, 1)
    spreader = (lane // HEAD_DIM == row).astype(f32)
    factors = contracted(factors, spreader, 0, 0, lax.Precision.HIGHEST)
    context = jnp.zeros((rows, columns), f32)
    for s in range(shards):
        context += factors[:, s * columns : (s + 1) * columns] * parts[s][:rows, :].astype(f32)
    out[...] = product(context.astype(bf16), weight[p]).astype(bf16)


def updated(state, parts):
    return state[...] + sum(parts[h].astype(f32) for h in range(parts.shape[0]))


def project_kernel(p, scale, state, parts, query_w, key_w, value_w, new_state, query, both):
    value = updated(state, parts)
    new_state[...] = value
    value = normed(value)
    columns = query_w.shape[2]
    query[...] = (product(value, query_w[p]) * scale).astype(bf16)
    both[:, :columns] = product(value, key_w[p]).astype(bf16)
    both[:, columns:] = product(value, value_w[p]).astype(bf16)


def attend_kernel(p, query, *refs):
    blocks, weight, out = refs[:-2], refs[-2], refs[-1]
    rows, columns = query.shape
    heads = columns // HEAD_DIM
    lane_head = lax.broadcasted_iota(jnp.int32, (rows, columns), 1) // HEAD_DIM
    some = query[...]
    stacked = [jnp.where(lane_head == h, some, jnp.zeros_like(some)) for h in range(heads)]
    stacked = jnp.concatenate(stacked, axis=0)
    scores = [contracted(block[:, :columns], stacked, 1, 1) for block in blocks]
    top = functools.reduce(jnp.maximum, scores)
    top = jnp.max(top, axis=0, keepdims=True)
    terms = [jnp.exp(part - top) for part in scores]
    total = jnp.sum(sum(terms), axis=0, keepdims=True)
    share = jnp.concatenate([(part / total).astype(bf16) for part in terms], axis=0)
    values = jnp.concatenate([block[:, columns:] for block in blocks], axis=0)
    made = contracted(share, values, 0, 0)
    context = jnp.zeros((rows, columns), f32)
    for h in range(heads):
        context = jnp.where(lane_head == h, made[h * rows : (h + 1) * rows, :], context)
    out[...] = product(context.astype(bf16), weight[p]).astype(bf16)


def mlp_kernel(p, state, parts, in_w, out_w, new_state, out):
    value = updated(state, parts)
    new_state[...] = value
    hidden = product(normed(value), in_w[p])
    hidden = 0.5 * hidden * (1.0 + lax.erf(hidden * 0.5**0.5))
    out[...] = product(hidden.astype(bf16), out_w[p]).astype(bf16)


def query_kernel(p, scale, state, parts, query_w, index, new_state, message):
    value = updated(state, parts)
    new_state[...] = value
    columns = query_w.shape[2]
    message[:, :columns] = (product(normed(value), query_w[p]) * scale).astype(bf16)
    own = new_state[:, pl.ds(pl.multiple_of(index[0, 0] * columns, columns), columns)]
    message[:, columns:] = own.astype(bf16)


def final_kernel(count, state, parts, share, other_share, me, new_state, midway):
    new_state[...] = updated(state, parts)
    rows = new_state.shape[0]
    line, side = me[0, 0] // 2, lax.rem(me[0, 0], 2)
    for k in range(count // 2):
        place_of = 2 * origin(count // 2, WIDEST // 2, k, line)
        for block, at in ((share, place_of + side), (other_share, place_of + 1 - side)):
            start = pl.multiple_of(at * rows, rows)
            midway[pl.ds(start, rows), :] = block[k * rows : (k + 1) * rows, :].astype(f32)


def local(
    frames,
    latents,
    cross_query,
    cross_key,
    cross_value,
    cross_out,
    self_query,
    self_key,
    self_value,
    self_out,
    mlp_in,
    mlp_out,
):
    scale = 1.0 / HEAD_DIM**0.5
    passes, width, columns = cross_query.shape
    shards, me = lax.axis_size("frames"), lax.axis_index("frames")
    latent_count = latents.shape[0]
    rows = latent_count // shards
    stat_rows = -(-STATS * (columns // HEAD_DIM) // 16) * 16
    state_shape = shaped((rows, width), f32)
    part_shape = shaped((rows, width), bf16)
    row_shape = shaped((rows, columns), bf16)
    double_shape = shaped((rows, 2 * columns), bf16)
    packed_shape = shaped((rows + stat_rows, columns), bf16)
    state, queries = whole_call(
        functools.partial(latents_kernel, scale, shards),
        (state_shape, shaped((latent_count, columns), bf16)),
        latents,
        cross_query,
        scalars=(me,),
        scratch=[pltpu.VMEM((latent_count, width), bf16)],
        cost=pl.CostEstimate(
            flops=2 * latent_count * width * columns,
            bytes_accessed=2 * latent_count * width,
            transcendentals=0,
        ),
    )
    frame_count = frames.shape[0]
    chunks = CHUNKS if frame_count % (CHUNKS * 256) == 0 else 1
    part_rows = frame_count // chunks
    count, side = lax.axis_size("heads"), lax.axis_index("heads")
    steps = range(2, count, 2)
    owners = [side, side ^ 1] + [(side - k) % count for k in steps]
    owners = owners + [((side ^ 1) - k) % count for k in steps]
    far = [
        [
            shifted(lax.slice_in_dim(frames, c * part_rows, (c + 1) * part_rows, axis=0), "heads", k)
            for k in steps
        ]
        for c in range(chunks)
    ]
    near = [frames, lax.ppermute(frames, "heads", [(i, i ^ 1) for i in range(count)])]
    chunk_shapes = (
        shaped((part_rows, width), bf16),
        shaped((part_rows, columns), bf16),
        shaped((columns, part_rows), bf16),
    )
    pieces = []
    for c in range(chunks):
        if c == 0:
            blocks, queries = pass_on(far[c], queries)
        else:
            blocks, pieces[-1] = pass_on(far[c], pieces[-1])
        piece = whole_call(
            functools.partial(frames_kernel, c),
            chunk_shapes,
            cross_key,
            cross_value,
            *near,
            *blocks,
            scalars=owners,
            cost=pl.CostEstimate(
                flops=4 * part_rows * width * columns,
                bytes_accessed=2 * part_rows * width,
                transcendentals=0,
            ),
        )
        pieces.append(piece)
    key_values = [None] + [
        whole_call(
            functools.partial(key_value_kernel, p),
            (shaped((frame_count, columns), bf16), shaped((columns, frame_count), bf16)),
            *[piece[0] for piece in pieces],
            cross_key,
            cross_value,
            cost=pl.CostEstimate(
                flops=4 * frame_count * width * columns,
                bytes_accessed=2 * frame_count * width,
                transcendentals=0,
            ),
        )
        for p in range(1, passes)
    ]
    heads = columns // HEAD_DIM
    carry_shapes = (shaped((columns, latent_count), f32), shaped((2 * heads, latent_count), f32))
    queries_cost = pl.CostEstimate(
        flops=4 * latent_count * part_rows * columns,
        bytes_accessed=4 * latent_count * columns,
        transcendentals=heads * latent_count * part_rows,
    )
    carry = ()
    for c, (_, keys, values) in enumerate(pieces):
        last = c + 1 == chunks
        carry = whole_call(
            functools.partial(partial_kernel, 1, 1, rows, c > 0, last),
            [packed_shape] * shards if last else carry_shapes,
            queries,
            keys,
            values,
            *carry,
            cost=queries_cost,
        )
    first_parts = returned_blocks(carry, "frames")
    for p in range(passes):
        if p == 0:
            parts = first_parts
        else:
            keys, values = key_values[p]
            results = [packed_shape] * len(queries) + [shaped((rows * len(queries), columns), bf16)]
            *parts, share = whole_call(
                functools.partial(partial_kernel, len(queries), 2, rows, False, True),
                results,
                *queries,
                keys,
                pair_swap(keys),
                values,
                pair_swap(values),
            )
            parts = line_return(parts)
            if p == 1:
                first_share = share
        part = whole_call(functools.partial(merge_kernel, p), part_shape, *parts, cross_out)
        state, query, both = whole_call(
            functools.partial(project_kernel, p, scale),
            (state_shape, row_shape, double_shape),
            state,
            lax.all_gather(part, "heads"),
            self_query,
            self_key,
            self_value,
        )
        blocks = gathered_blocks(both, "frames")
        part = whole_call(functools.partial(attend_kernel, p), part_shape, query, *blocks, self_out)
        state, part = whole_call(
            functools.partial(mlp_kernel, p),
            (state_shape, part_shape),
            state,
            lax.all_gather(part, "heads"),
            mlp_in,
            mlp_out,
        )
        part = lax.all_gather(part, "heads")
        if p + 1 < passes:
            state, message = whole_call(
                functools.partial(query_kernel, p + 1, scale),
                (state_shape, double_shape),
                state,
                part,
                cross_query,
                scalars=(lax.axis_index("heads"),),
            )
            queries = line_gather(message)
        else:
            state, midway = whole_call(
                functools.partial(final_kernel, shards),
                (state_shape, shaped((latent_count, columns), f32)),
                state,
                part,
                first_share,
                pair_swap(first_share),
                scalars=(me,),
            )
    return (state, midway)


def solution(mesh):
    columns, rows = P(None, None, "heads"), P(None, "heads", None)
    placed = (P("frames", "heads"), P(), columns, columns, columns, rows)
    placed = placed + (columns, columns, columns, rows, columns, rows)
    return jax.shard_map(
        local,
        mesh=mesh,
        in_specs=placed,
        out_specs=(P("frames", None), P(None, "heads")),
        check_vma=False,
    )
```

```python
import functools

import jax
import jax.numpy as jnp
from jax import lax
from jax.experimental import pallas as pl
from jax.experimental.pallas import tpu as pltpu
from jax.sharding import PartitionSpec as P

HEAD_DIM = 64
STATS = 4
VMEM_BYTES = 10 << 20
LOAD_BYTES = 51 << 20
CHUNKS = 2
WIDEST = 8
epsilon = 1e-05
f32, bf16 = jnp.float32, jnp.bfloat16


def shifted(value, axis, step):
    count = lax.axis_size(axis)
    return lax.ppermute(value, axis, [(i, (i + step) % count) for i in range(count)])


def origin(count, widest, k, me):
    return k if count > widest else lax.rem(me - k + count, count)


def gathered_blocks(value, axis):
    count = lax.axis_size(axis)
    if count > WIDEST:
        pieces = lax.all_gather(value, axis)
        return [pieces[k] for k in range(count)]
    return [value] + [shifted(value, axis, k) for k in range(1, count)]


def line_of(count):
    return [list(range(x, count, 2)) for x in range(2)]


def line_shift(value, step):
    count = lax.axis_size("frames")
    return lax.ppermute(value, "frames", [(i, (i + 2 * step) % count) for i in range(count)])


def line_gather(value):
    count = lax.axis_size("frames")
    if count > WIDEST:
        pieces = lax.all_gather(value, "frames", axis_index_groups=line_of(count))
        return [pieces[k] for k in range(count // 2)]
    return [value] + [line_shift(value, k) for k in range(1, count // 2)]


def line_return(blocks):
    count = lax.axis_size("frames")
    if count > WIDEST:
        groups = line_of(count)
        pieces = lax.all_to_all(jnp.stack(blocks), "frames", 0, 0, axis_index_groups=groups)
        return [pieces[k] for k in range(count // 2)]
    return [blocks[0]] + [line_shift(blocks[k], -k) for k in range(1, count // 2)]


def pair_swap(value):
    count = lax.axis_size("frames")
    return lax.ppermute(value, "frames", [(i, i ^ 1) for i in range(count)])


def pass_on(blocks, alongside):
    count = lax.axis_size("heads")
    blocks, alongside = lax.optimization_barrier((blocks, alongside))
    swap = [(i, i ^ 1) for i in range(count)]
    return blocks + [lax.ppermute(block, "heads", swap) for block in blocks], alongside


def whole_call(body, results, *operands, cost=None, unplaced=(), scalars=(), after=(), scratch=(), limit=None):
    space = pl.BlockSpec(memory_space=pltpu.VMEM)
    specs = [pl.BlockSpec(memory_space=pltpu.HBM)] * len(unplaced) + [space] * len(operands)
    specs += [pl.BlockSpec(memory_space=pltpu.SMEM)] * len(scalars) + [space] * len(after)
    scalars = [jnp.asarray(index, jnp.int32).reshape(1, 1) for index in scalars]
    return pl.pallas_call(
        body,
        out_shape=results,
        in_specs=specs,
        out_specs=jax.tree.map(lambda _: space, results),
        scratch_shapes=scratch,
        compiler_params=pltpu.CompilerParams(vmem_limit_bytes=limit or VMEM_BYTES),
        cost_estimate=cost,
    )(*unplaced, *operands, *scalars, *after)


def shaped(shape, dtype):
    return jax.ShapeDtypeStruct(shape, dtype)


def normed(vector):
    centre = vector - jnp.mean(vector, axis=-1, keepdims=True)
    spread_sq = jnp.mean(centre * centre, axis=-1, keepdims=True)
    return (centre * lax.rsqrt(spread_sq + epsilon)).astype(bf16)


def product(left_side, weight):
    return jnp.dot(left_side, weight, preferred_element_type=f32)


def contracted(left_side, right_side, left_dim, right_dim, precision=None):
    return lax.dot_general(
        left_side,
        right_side,
        (((left_dim,), (right_dim,)), ((), ())),
        precision=precision,
        preferred_element_type=f32,
    )


def chunk_kernel(chunk, count, first_half, carried, *refs):
    queries, key_w, value_w = refs[:3]
    blocks, owners, refs = refs[3 : 3 + count], refs[3 + count : 3 + 2 * count], refs[3 + 2 * count :]
    carry, outs = (refs[:2], refs[2:]) if carried else (None, refs)
    out, keys, values = outs[:3]
    rows, width = out.shape[0], blocks[0].shape[1]
    served = queries.at[pl.ds(first_half, queries.shape[0] - first_half), :]
    tile = min(rows, 32)
    for start in range(0, rows, tile):
        pieces = []
        for block in blocks:
            first = start + (chunk * rows if block.shape[0] > rows else 0)
            pieces.append(block[first : first + tile, :].astype(f32))
        mean = jnp.sum(sum(pieces), axis=1, keepdims=True) / (width * count)
        pieces = [piece - mean for piece in pieces]
        total = jnp.sum(sum(piece * piece for piece in pieces), axis=1, keepdims=True)
        scale = lax.rsqrt(total / (width * count) + epsilon)
        for piece, owner in zip(pieces, owners):
            lanes = pl.ds(pl.multiple_of(owner[0, 0] * width, width), width)
            out[start : start + tile, lanes] = (piece * scale).astype(bf16)
    keys[...] = product(out[...], key_w[...]).astype(bf16)
    values[...] = product(out[...], value_w[...]).astype(bf16).T
    for found in weighed(served, [keys], [values], carry, first_half):
        if first_half:
            store_terms(outs[3], *found)
        else:
            store_carry(outs[3], outs[4], *found)


def own_kernel(queries, keys, values, carry_out, carry_stats, out, stats):
    served = queries.at[pl.ds(0, out.shape[1]), :]
    for found in weighed(served, [keys], [values], (carry_out, carry_stats), 0):
        store_carry(out, stats, *found)


def key_value_kernel(p, *refs):
    row_refs, (key_w, value_w, keys, values) = refs[:-4], refs[-4:]
    start = 0
    for rows in row_refs:
        end = start + rows.shape[0]
        keys[start:end, :] = product(rows[...], key_w[p]).astype(bf16)
        values[:, start:end] = product(rows[...], value_w[p]).astype(bf16).T
        start = end


def latents_kernel(scale, count, frames_hbm, key_hbm, value_hbm, latents_hbm, query_hbm, me, *refs):
    state, queries, own, key_w, value_w, latents, query_w, rows_normed, sems = refs
    moves = [
        (latents_hbm, latents),
        (query_hbm.at[0], query_w),
        (frames_hbm, own),
        (key_hbm.at[0], key_w),
        (value_hbm.at[0], value_w),
    ]
    loads = [pltpu.make_async_copy(*move, sems.at[i]) for i, move in enumerate(moves)]
    for load in loads:
        load.start()
    rows = state.shape[0]
    line, side = me[0, 0] // 2, lax.rem(me[0, 0], 2)
    loads[0].wait()
    for j in range(count):
        k = j % (count // 2)
        index = 2 * origin(count // 2, WIDEST // 2, k, line) + (side if j == k else 1 - side)
        value = latents[pl.ds(pl.multiple_of(index * rows, rows), rows), :].astype(f32)
        rows_normed[j * rows : (j + 1) * rows, :] = normed(value)
    state[...] = latents[pl.ds(pl.multiple_of(me[0, 0] * rows, rows), rows), :].astype(f32)
    loads[1].wait()
    queries[...] = (product(rows_normed[...], query_w[...]) * scale).astype(bf16)
    for load in loads[2:]:
        load.wait()


def split_terms(value):
    high = value.astype(bf16).astype(f32)
    return high, (value - high).astype(bf16).astype(f32)


def weighed(queries, key_refs, value_refs, carry, carry_start):
    columns = key_refs[0].shape[1]
    latents = queries.shape[0]
    heads = columns // HEAD_DIM
    chunk = min(latents, 256)
    span = min(columns, 128)
    lane_head = lax.broadcasted_iota(jnp.int32, (chunk, span), 1) // HEAD_DIM

    def scores_of(start, h):
        lanes = slice(h * HEAD_DIM // span * span, (h * HEAD_DIM // span + 1) * span)
        some = queries[start : start + chunk, lanes]
        mine = lane_head == h % (span // HEAD_DIM)
        one = jnp.where(mine, some, jnp.zeros_like(some))
        return [contracted(keys[:, lanes], one, 1, 1) for keys in key_refs]

    order = [(start, h) for start in range(0, latents, chunk) for h in range(heads)]
    coming = scores_of(*order[0])
    for start in range(0, latents, chunk):
        pieces, tops, sums = [], [], []
        for h in range(heads):
            scores, following = coming, order.index((start, h)) + 1
            if following < len(order):
                coming = scores_of(*order[following])
            top = functools.reduce(
                jnp.maximum, [jnp.max(part, axis=0, keepdims=True) for part in scores]
            )
            own = slice(h * HEAD_DIM, (h + 1) * HEAD_DIM)
            place = slice(carry_start + start, carry_start + start + chunk)
            if carry is not None:
                before = carry[1][h : h + 1, place]
                top = jnp.maximum(top, before)
            high, low = split_terms(top)
            top = high + low
            terms = [jnp.exp(part - top) for part in scores]
            total = sum(jnp.sum(part, axis=0, keepdims=True) for part in terms)
            piece = sum(product(v[own, :], part.astype(bf16)) for v, part in zip(value_refs, terms))
            if carry is not None:
                factor = jnp.exp(before - top)
                total += factor * carry[1][heads + h : heads + h + 1, place]
                piece += factor * carry[0][own, place]
            pieces.append(piece)
            tops.append(top)
            sums.append(total)
        yield start, pieces, tops, sums


def store_carry(out, stats, start, pieces, tops, sums):
    for h, rows in enumerate(tops + sums):
        stats[h : h + 1, start : start + rows.shape[1]] = rows
    for h, piece in enumerate(pieces):
        out[h * HEAD_DIM : (h + 1) * HEAD_DIM, start : start + piece.shape[1]] = piece


def split_stats(tops, sums, count):
    tops, sums = [split_terms(top) for top in tops], [split_terms(total) for total in sums]
    rows = [pair[0] for pair in tops] + [pair[1] for pair in tops]
    rows += [pair[0] for pair in sums] + [pair[1] for pair in sums]
    rows += [jnp.zeros_like(rows[0])] * (count - len(rows))
    return jnp.concatenate(rows, axis=0)


def joined_stats(stats, heads):
    return stats[:heads] + stats[heads : 2 * heads], stats[2 * heads : 3 * heads] + stats[3 * heads : 4 * heads]


def store_terms(out, start, pieces, tops, sums):
    place = slice(start, start + pieces[0].shape[1])
    columns = len(pieces) * HEAD_DIM
    out[:columns, place] = jnp.concatenate(pieces, axis=0).astype(bf16)
    out[columns:, place] = split_stats(tops, sums, out.shape[0] - columns).astype(bf16)


def store_packed(outs, rows, start, pieces, tops, sums):
    columns = len(pieces) * HEAD_DIM
    turned = jnp.concatenate(pieces, axis=0).T.astype(bf16)
    stats = split_stats(tops, sums, outs[0].shape[0] - rows)
    for j in range(turned.shape[0] // rows):
        out = outs[start // rows + j]
        out[:rows, :] = turned[j * rows : (j + 1) * rows, :]
        piece = stats[:, j * rows : (j + 1) * rows]
        piece = jnp.concatenate([piece, jnp.zeros((piece.shape[0], columns - rows), f32)], axis=1)
        out[rows:, :] = piece.astype(bf16)


def fold_kernel(rows, carry_out, carry_stats, other, *outs):
    columns, _ = carry_out.shape
    heads = columns // HEAD_DIM
    tops, sums = carry_stats[:heads, :], carry_stats[heads:, :]
    other_tops, other_sums = joined_stats(other[columns:, :].astype(f32), heads)
    highest = jnp.maximum(tops, other_tops)
    factor, other_factor = jnp.exp(tops - highest), jnp.exp(other_tops - highest)
    total = factor * sums + other_factor * other_sums
    pieces = []
    for h in range(heads):
        own = slice(h * HEAD_DIM, (h + 1) * HEAD_DIM)
        piece = factor[h : h + 1] * carry_out[own, :]
        pieces.append(piece + other_factor[h : h + 1] * other[own, :].astype(f32))
    tops = [highest[h : h + 1] for h in range(heads)]
    sums = [total[h : h + 1] for h in range(heads)]
    store_packed(outs, rows, 0, pieces, tops, sums)


def partial_kernel(query_count, rows, *refs):
    query_refs, refs = refs[:query_count], refs[query_count:]
    key_refs, value_refs, outs, share = refs[:2], refs[2:4], refs[4:-1], refs[-1]
    columns = key_refs[0].shape[1]
    queries = jnp.concatenate([ref[:, :columns] for ref in query_refs], axis=0)
    for k, ref in enumerate(query_refs):
        share[k * rows : (k + 1) * rows, :] = ref[:, columns:]
    for found in weighed(queries, key_refs, value_refs, None, 0):
        store_packed(outs, rows, *found)


def merge_kernel(p, *refs):
    parts, weight, out = refs[:-2], refs[-2], refs[-1]
    shards, columns = len(parts), parts[0].shape[1]
    heads = columns // HEAD_DIM
    rows = out.shape[0]
    tops, sums = [], []
    for s in range(shards):
        top, total = joined_stats(parts[s][rows:, :].astype(f32)[:, :rows], heads)
        tops.append(top)
        sums.append(total)
    highest = functools.reduce(jnp.maximum, tops)
    factors = [jnp.exp(top - highest) for top in tops]
    total = sum(factor * one for factor, one in zip(factors, sums))
    factors = jnp.concatenate([factor / total for factor in factors], axis=0)
    shape = (shards * heads, shards * columns)
    row = lax.broadcasted_iota(jnp.int32, shape, 0)
    lane = lax.broadcasted_iota(jnp.int32, shape, 1)
    spreader = (lane // HEAD_DIM == row).astype(f32)
    factors = contracted(factors, spreader, 0, 0, lax.Precision.HIGHEST)
    context = jnp.zeros((rows, columns), f32)
    for s in range(shards):
        context += factors[:, s * columns : (s + 1) * columns] * parts[s][:rows, :].astype(f32)
    out[...] = product(context.astype(bf16), weight[p]).astype(bf16)


def updated(state, parts):
    return state[...] + sum(parts[h].astype(f32) for h in range(parts.shape[0]))


def project_kernel(p, scale, state, parts, query_w, key_w, value_w, new_state, query, both):
    value = updated(state, parts)
    new_state[...] = value
    value = normed(value)
    columns = query_w.shape[2]
    query[...] = (product(value, query_w[p]) * scale).astype(bf16)
    both[:, :columns] = product(value, key_w[p]).astype(bf16)
    both[:, columns:] = product(value, value_w[p]).astype(bf16)


def attend_kernel(p, query, *refs):
    blocks, weight, out = refs[:-2], refs[-2], refs[-1]
    rows, columns = query.shape
    heads = columns // HEAD_DIM
    lane_head = lax.broadcasted_iota(jnp.int32, (rows, columns), 1) // HEAD_DIM
    some = query[...]
    stacked = [jnp.where(lane_head == h, some, jnp.zeros_like(some)) for h in range(heads)]
    stacked = jnp.concatenate(stacked, axis=0)
    scores = [contracted(block[:, :columns], stacked, 1, 1) for block in blocks]
    top = functools.reduce(jnp.maximum, scores)
    top = jnp.max(top, axis=0, keepdims=True)
    terms = [jnp.exp(part - top) for part in scores]
    total = jnp.sum(sum(terms), axis=0, keepdims=True)
    share = jnp.concatenate([(part / total).astype(bf16) for part in terms], axis=0)
    values = jnp.concatenate([block[:, columns:] for block in blocks], axis=0)
    made = contracted(share, values, 0, 0)
    context = jnp.zeros((rows, columns), f32)
    for h in range(heads):
        context = jnp.where(lane_head == h, made[h * rows : (h + 1) * rows, :], context)
    out[...] = product(context.astype(bf16), weight[p]).astype(bf16)


def mlp_kernel(p, state, parts, in_w, out_w, new_state, out):
    value = updated(state, parts)
    new_state[...] = value
    hidden = product(normed(value), in_w[p])
    hidden = 0.5 * hidden * (1.0 + lax.erf(hidden * 0.5**0.5))
    out[...] = product(hidden.astype(bf16), out_w[p]).astype(bf16)


def query_kernel(p, scale, state, parts, query_w, index, new_state, message):
    value = updated(state, parts)
    new_state[...] = value
    columns = query_w.shape[2]
    message[:, :columns] = (product(normed(value), query_w[p]) * scale).astype(bf16)
    own = new_state[:, pl.ds(pl.multiple_of(index[0, 0] * columns, columns), columns)]
    message[:, columns:] = own.astype(bf16)


def final_kernel(count, state, parts, share, other_share, me, new_state, midway):
    new_state[...] = updated(state, parts)
    rows = new_state.shape[0]
    line, side = me[0, 0] // 2, lax.rem(me[0, 0], 2)
    for k in range(count // 2):
        place_of = 2 * origin(count // 2, WIDEST // 2, k, line)
        for block, at in ((share, place_of + side), (other_share, place_of + 1 - side)):
            start = pl.multiple_of(at * rows, rows)
            midway[pl.ds(start, rows), :] = block[k * rows : (k + 1) * rows, :].astype(f32)


def local(
    frames,
    latents,
    cross_query,
    cross_key,
    cross_value,
    cross_out,
    self_query,
    self_key,
    self_value,
    self_out,
    mlp_in,
    mlp_out,
):
    scale = 1.0 / HEAD_DIM**0.5
    passes, width, columns = cross_query.shape
    shards, me = lax.axis_size("frames"), lax.axis_index("frames")
    latent_count = latents.shape[0]
    rows = latent_count // shards
    stat_rows = -(-STATS * (columns // HEAD_DIM) // 16) * 16
    state_shape = shaped((rows, width), f32)
    part_shape = shaped((rows, width), bf16)
    row_shape = shaped((rows, columns), bf16)
    double_shape = shaped((rows, 2 * columns), bf16)
    packed_shape = shaped((rows + stat_rows, columns), bf16)
    state, queries, own, key_w, value_w = whole_call(
        functools.partial(latents_kernel, scale, shards),
        (
            state_shape,
            shaped((latent_count, columns), bf16),
            shaped(frames.shape, bf16),
            shaped((width, columns), bf16),
            shaped((width, columns), bf16),
        ),
        unplaced=(frames, cross_key, cross_value, latents, cross_query),
        scalars=(me,),
        scratch=[
            pltpu.VMEM((latent_count, width), bf16),
            pltpu.VMEM((width, columns), bf16),
            pltpu.VMEM((latent_count, width), bf16),
            pltpu.SemaphoreType.DMA((5,)),
        ],
        limit=LOAD_BYTES,
        cost=pl.CostEstimate(
            flops=2 * latent_count * width * columns,
            bytes_accessed=2 * latent_count * width,
            transcendentals=0,
        ),
    )
    frame_count = frames.shape[0]
    chunks = CHUNKS
    part_rows = frame_count // chunks
    count, side = lax.axis_size("heads"), lax.axis_index("heads")
    steps = range(2, count, 2)
    owners = [side, side ^ 1] + [(side - k) % count for k in steps]
    owners = owners + [((side ^ 1) - k) % count for k in steps]
    far = []
    for c in range(chunks):
        piece = lax.slice_in_dim(frames, c * part_rows, (c + 1) * part_rows, axis=0)
        far.append([shifted(piece, "heads", k) for k in steps])
    near = lax.ppermute(frames, "heads", [(i, i ^ 1) for i in range(count)])
    heads = columns // HEAD_DIM
    line_latents = latent_count // 2
    line_shape = shaped((columns + stat_rows, line_latents), bf16)
    results = [
        shaped((part_rows, width), bf16),
        shaped((part_rows, columns), bf16),
        shaped((columns, part_rows), bf16),
    ]

    def carry_of(latent_rows):
        return [shaped((columns, latent_rows), f32), shaped((2 * heads, latent_rows), f32)]

    pieces, carry = [], []
    for c in range(chunks):
        last = c + 1 == chunks
        served = line_latents if last else latent_count
        if c == 0:
            blocks, queries = pass_on(far[c], queries)
        else:
            blocks, pieces[-1] = pass_on(far[c], pieces[-1])
        made = whole_call(
            functools.partial(chunk_kernel, c, count, line_latents if last else 0, c > 0),
            results + ([line_shape] if last else carry_of(latent_count)),
            queries,
            key_w,
            value_w,
            own,
            near,
            *blocks,
            scalars=owners,
            after=carry,
            cost=pl.CostEstimate(
                flops=4 * part_rows * width * columns,
                bytes_accessed=2 * part_rows * width,
                transcendentals=heads * served * part_rows,
            ),
        )
        pieces.append(made[:3])
        if not last:
            carry = made[3:]
    other = pair_swap(made[3])
    carry = whole_call(
        own_kernel,
        carry_of(line_latents),
        queries,
        *made[1:3],
        *carry,
        cost=pl.CostEstimate(
            flops=4 * line_latents * part_rows * columns,
            bytes_accessed=4 * latent_count * columns,
            transcendentals=heads * line_latents * part_rows,
        ),
    )
    line_count = shards // 2
    first_parts = whole_call(
        functools.partial(fold_kernel, rows), [packed_shape] * line_count, *carry, other
    )
    key_values = [None] + [
        whole_call(
            functools.partial(key_value_kernel, p),
            (shaped((frame_count, columns), bf16), shaped((columns, frame_count), bf16)),
            *[piece[0] for piece in pieces],
            cross_key,
            cross_value,
            cost=pl.CostEstimate(
                flops=4 * frame_count * width * columns,
                bytes_accessed=2 * frame_count * width,
                transcendentals=0,
            ),
        )
        for p in range(1, passes)
    ]
    for p in range(passes):
        if p == 0:
            parts = line_return(first_parts)
        else:
            keys, values = key_values[p]
            results = [packed_shape] * len(queries) + [shaped((rows * len(queries), columns), bf16)]
            *parts, share = whole_call(
                functools.partial(partial_kernel, len(queries), rows),
                results,
                *queries,
                keys,
                pair_swap(keys),
                values,
                pair_swap(values),
            )
            parts = line_return(parts)
            if p == 1:
                first_share = share
        part = whole_call(functools.partial(merge_kernel, p), part_shape, *parts, cross_out)
        state, query, both = whole_call(
            functools.partial(project_kernel, p, scale),
            (state_shape, row_shape, double_shape),
            state,
            lax.all_gather(part, "heads"),
            self_query,
            self_key,
            self_value,
        )
        if shards > WIDEST:
            blocks = gathered_blocks(both, "frames")
        else:
            blocks = line_gather(both)
            blocks = blocks + [pair_swap(block) for block in blocks]
        part = whole_call(functools.partial(attend_kernel, p), part_shape, query, *blocks, self_out)
        state, part = whole_call(
            functools.partial(mlp_kernel, p),
            (state_shape, part_shape),
            state,
            lax.all_gather(part, "heads"),
            mlp_in,
            mlp_out,
        )
        part = lax.all_gather(part, "heads")
        if p + 1 < passes:
            state, message = whole_call(
                functools.partial(query_kernel, p + 1, scale),
                (state_shape, double_shape),
                state,
                part,
                cross_query,
                scalars=(lax.axis_index("heads"),),
            )
            queries = line_gather(message)
        else:
            state, midway = whole_call(
                functools.partial(final_kernel, shards),
                (state_shape, shaped((latent_count, columns), f32)),
                state,
                part,
                first_share,
                pair_swap(first_share),
                scalars=(me,),
            )
    return (state, midway)


def solution(mesh):
    columns, rows = P(None, None, "heads"), P(None, "heads", None)
    placed = (P("frames", "heads"), P(), columns, columns, columns, rows)
    placed = placed + (columns, columns, columns, rows, columns, rows)
    return jax.shard_map(
        local,
        mesh=mesh,
        in_specs=placed,
        out_specs=(P("frames", None), P(None, "heads")),
        check_vma=False,
    )
```

```python
import functools

import jax
import jax.numpy as jnp
from jax import lax
from jax.experimental import pallas as pl
from jax.experimental.pallas import tpu as pltpu
from jax.sharding import PartitionSpec as P

HEAD_DIM = 64
STATS = 4
VMEM_BYTES = 10 << 20
LOAD_BYTES = 51 << 20
CHUNKS = 2
WIDEST = 8
epsilon = 1e-05
f32, bf16 = jnp.float32, jnp.bfloat16


def shifted(value, axis, step):
    count = lax.axis_size(axis)
    return lax.ppermute(value, axis, [(i, (i + step) % count) for i in range(count)])


def origin(count, widest, k, me):
    return k if count > widest else lax.rem(me - k + count, count)


def gathered_blocks(value, axis):
    count = lax.axis_size(axis)
    if count > WIDEST:
        pieces = lax.all_gather(value, axis)
        return [pieces[k] for k in range(count)]
    return [value] + [shifted(value, axis, k) for k in range(1, count)]


def line_of(count):
    return [list(range(x, count, 2)) for x in range(2)]


def line_shift(value, step):
    count = lax.axis_size("frames")
    return lax.ppermute(value, "frames", [(i, (i + 2 * step) % count) for i in range(count)])


def line_gather(value):
    count = lax.axis_size("frames")
    if count > WIDEST:
        pieces = lax.all_gather(value, "frames", axis_index_groups=line_of(count))
        return [pieces[k] for k in range(count // 2)]
    return [value] + [line_shift(value, k) for k in range(1, count // 2)]


def line_return(blocks):
    count = lax.axis_size("frames")
    if count > WIDEST:
        groups = line_of(count)
        pieces = lax.all_to_all(jnp.stack(blocks), "frames", 0, 0, axis_index_groups=groups)
        return [pieces[k] for k in range(count // 2)]
    return [blocks[0]] + [line_shift(blocks[k], -k) for k in range(1, count // 2)]


def pair_swap(value):
    count = lax.axis_size("frames")
    return lax.ppermute(value, "frames", [(i, i ^ 1) for i in range(count)])


def pass_on(blocks, alongside):
    count = lax.axis_size("heads")
    blocks, alongside = lax.optimization_barrier((blocks, alongside))
    swap = [(i, i ^ 1) for i in range(count)]
    return blocks + [lax.ppermute(block, "heads", swap) for block in blocks], alongside


def whole_call(body, results, *operands, cost=None, unplaced=(), scalars=(), after=(), scratch=(), limit=None):
    space = pl.BlockSpec(memory_space=pltpu.VMEM)
    specs = [pl.BlockSpec(memory_space=pltpu.HBM)] * len(unplaced) + [space] * len(operands)
    specs += [pl.BlockSpec(memory_space=pltpu.SMEM)] * len(scalars) + [space] * len(after)
    scalars = [jnp.asarray(index, jnp.int32).reshape(1, 1) for index in scalars]
    return pl.pallas_call(
        body,
        out_shape=results,
        in_specs=specs,
        out_specs=jax.tree.map(lambda _: space, results),
        scratch_shapes=scratch,
        compiler_params=pltpu.CompilerParams(vmem_limit_bytes=limit or VMEM_BYTES),
        cost_estimate=cost,
    )(*unplaced, *operands, *scalars, *after)


def shaped(shape, dtype):
    return jax.ShapeDtypeStruct(shape, dtype)


def normed(vector):
    centre = vector - jnp.mean(vector, axis=-1, keepdims=True)
    spread_sq = jnp.mean(centre * centre, axis=-1, keepdims=True)
    return (centre * lax.rsqrt(spread_sq + epsilon)).astype(bf16)


def product(left_side, weight):
    return jnp.dot(left_side, weight, preferred_element_type=f32)


def contracted(left_side, right_side, left_dim, right_dim, precision=None):
    return lax.dot_general(
        left_side,
        right_side,
        (((left_dim,), (right_dim,)), ((), ())),
        precision=precision,
        preferred_element_type=f32,
    )


def chunk_kernel(chunk, count, first_half, carried, *refs):
    queries, key_w, value_w = refs[:3]
    blocks, owners, refs = refs[3 : 3 + count], refs[3 + count : 3 + 2 * count], refs[3 + 2 * count :]
    carry, outs = (refs[:2], refs[2:]) if carried else (None, refs)
    outs = outs if first_half else (outs[0], outs[3], outs[4], outs[1], outs[2])
    out, keys, values = outs[:3]
    rows, width = out.shape[0], blocks[0].shape[1]
    served = queries.at[pl.ds(first_half, queries.shape[0] - first_half), :]
    tile = min(rows, 32)
    for start in range(0, rows, tile):
        pieces = []
        for block in blocks:
            first = start + (chunk * rows if block.shape[0] > rows else 0)
            pieces.append(block[first : first + tile, :].astype(f32))
        mean = jnp.sum(sum(pieces), axis=1, keepdims=True) / (width * count)
        pieces = [piece - mean for piece in pieces]
        total = jnp.sum(sum(piece * piece for piece in pieces), axis=1, keepdims=True)
        scale = lax.rsqrt(total / (width * count) + epsilon)
        for piece, owner in zip(pieces, owners):
            lanes = pl.ds(pl.multiple_of(owner[0, 0] * width, width), width)
            out[start : start + tile, lanes] = (piece * scale).astype(bf16)
    keys[...] = product(out[...], key_w[...]).astype(bf16)
    values[...] = product(out[...], value_w[...]).astype(bf16).T
    for found in weighed(served, [keys], [values], carry, first_half):
        if first_half:
            store_terms(outs[3], *found)
        else:
            store_carry(outs[3], outs[4], *found)


def own_kernel(queries, keys, values, carry_out, carry_stats, out, stats):
    served = queries.at[pl.ds(0, out.shape[1]), :]
    for found in weighed(served, [keys], [values], (carry_out, carry_stats), 0):
        store_carry(out, stats, *found)


def key_value_kernel(p, *refs):
    row_refs, (key_w, value_w, keys, values) = refs[:-4], refs[-4:]
    start = 0
    for rows in row_refs:
        end = start + rows.shape[0]
        keys[start:end, :] = product(rows[...], key_w[p]).astype(bf16)
        values[:, start:end] = product(rows[...], value_w[p]).astype(bf16).T
        start = end


def latents_kernel(scale, count, frames_hbm, key_hbm, value_hbm, latents_hbm, query_hbm, me, *refs):
    state, queries, own, key_w, value_w, latents, query_w, rows_normed, sems = refs
    moves = [
        (latents_hbm, latents),
        (query_hbm.at[0], query_w),
        (frames_hbm, own),
        (key_hbm.at[0], key_w),
        (value_hbm.at[0], value_w),
    ]
    loads = [pltpu.make_async_copy(*move, sems.at[i]) for i, move in enumerate(moves)]
    for load in loads:
        load.start()
    rows = state.shape[0]
    line, side = me[0, 0] // 2, lax.rem(me[0, 0], 2)
    loads[0].wait()
    for j in range(count):
        k = j % (count // 2)
        index = 2 * origin(count // 2, WIDEST // 2, k, line) + (side if j == k else 1 - side)
        value = latents[pl.ds(pl.multiple_of(index * rows, rows), rows), :].astype(f32)
        rows_normed[j * rows : (j + 1) * rows, :] = normed(value)
    state[...] = latents[pl.ds(pl.multiple_of(me[0, 0] * rows, rows), rows), :].astype(f32)
    loads[1].wait()
    queries[...] = (product(rows_normed[...], query_w[...]) * scale).astype(bf16)
    for load in loads[2:]:
        load.wait()


def split_terms(value):
    high = value.astype(bf16).astype(f32)
    return high, (value - high).astype(bf16).astype(f32)


def weighed(queries, key_refs, value_refs, carry, carry_start):
    columns = key_refs[0].shape[1]
    latents = queries.shape[0]
    heads = columns // HEAD_DIM
    chunk = min(latents, 256)
    span = min(columns, 128)
    lane_head = lax.broadcasted_iota(jnp.int32, (chunk, span), 1) // HEAD_DIM

    def scores_of(start, h):
        lanes = slice(h * HEAD_DIM // span * span, (h * HEAD_DIM // span + 1) * span)
        some = queries[start : start + chunk, lanes]
        mine = lane_head == h % (span // HEAD_DIM)
        one = jnp.where(mine, some, jnp.zeros_like(some))
        return [contracted(keys[:, lanes], one, 1, 1) for keys in key_refs]

    order = [(start, h) for start in range(0, latents, chunk) for h in range(heads)]
    coming = scores_of(*order[0])
    for start in range(0, latents, chunk):
        pieces, tops, sums = [], [], []
        for h in range(heads):
            scores, following = coming, order.index((start, h)) + 1
            if following < len(order):
                coming = scores_of(*order[following])
            top = functools.reduce(
                jnp.maximum, [jnp.max(part, axis=0, keepdims=True) for part in scores]
            )
            own = slice(h * HEAD_DIM, (h + 1) * HEAD_DIM)
            place = slice(carry_start + start, carry_start + start + chunk)
            if carry is not None:
                before = carry[1][h : h + 1, place]
                top = jnp.maximum(top, before)
            high, low = split_terms(top)
            top = high + low
            terms = [jnp.exp(part - top) for part in scores]
            total = sum(jnp.sum(part, axis=0, keepdims=True) for part in terms)
            piece = sum(product(v[own, :], part.astype(bf16)) for v, part in zip(value_refs, terms))
            if carry is not None:
                factor = jnp.exp(before - top)
                total += factor * carry[1][heads + h : heads + h + 1, place]
                piece += factor * carry[0][own, place]
            pieces.append(piece)
            tops.append(top)
            sums.append(total)
        yield start, pieces, tops, sums


def store_carry(out, stats, start, pieces, tops, sums):
    for h, rows in enumerate(tops + sums):
        stats[h : h + 1, start : start + rows.shape[1]] = rows
    for h, piece in enumerate(pieces):
        out[h * HEAD_DIM : (h + 1) * HEAD_DIM, start : start + piece.shape[1]] = piece


def split_stats(tops, sums, count):
    tops, sums = [split_terms(top) for top in tops], [split_terms(total) for total in sums]
    rows = [pair[0] for pair in tops] + [pair[1] for pair in tops]
    rows += [pair[0] for pair in sums] + [pair[1] for pair in sums]
    rows += [jnp.zeros_like(rows[0])] * (count - len(rows))
    return jnp.concatenate(rows, axis=0)


def joined_stats(stats, heads):
    return stats[:heads] + stats[heads : 2 * heads], stats[2 * heads : 3 * heads] + stats[3 * heads : 4 * heads]


def store_terms(out, start, pieces, tops, sums):
    place = slice(start, start + pieces[0].shape[1])
    columns = len(pieces) * HEAD_DIM
    out[:columns, place] = jnp.concatenate(pieces, axis=0).astype(bf16)
    out[columns:, place] = split_stats(tops, sums, out.shape[0] - columns).astype(bf16)


def store_packed(outs, rows, start, pieces, tops, sums):
    columns = len(pieces) * HEAD_DIM
    turned = jnp.concatenate(pieces, axis=0).T.astype(bf16)
    stats = split_stats(tops, sums, outs[0].shape[0] - rows)
    for j in range(turned.shape[0] // rows):
        out = outs[start // rows + j]
        out[:rows, :] = turned[j * rows : (j + 1) * rows, :]
        piece = stats[:, j * rows : (j + 1) * rows]
        piece = jnp.concatenate([piece, jnp.zeros((piece.shape[0], columns - rows), f32)], axis=1)
        out[rows:, :] = piece.astype(bf16)


def fold_kernel(rows, carry_out, carry_stats, other, *outs):
    columns, _ = carry_out.shape
    heads = columns // HEAD_DIM
    tops, sums = carry_stats[:heads, :], carry_stats[heads:, :]
    other_tops, other_sums = joined_stats(other[columns:, :].astype(f32), heads)
    highest = jnp.maximum(tops, other_tops)
    factor, other_factor = jnp.exp(tops - highest), jnp.exp(other_tops - highest)
    total = factor * sums + other_factor * other_sums
    pieces = []
    for h in range(heads):
        own = slice(h * HEAD_DIM, (h + 1) * HEAD_DIM)
        piece = factor[h : h + 1] * carry_out[own, :]
        pieces.append(piece + other_factor[h : h + 1] * other[own, :].astype(f32))
    tops = [highest[h : h + 1] for h in range(heads)]
    sums = [total[h : h + 1] for h in range(heads)]
    store_packed(outs, rows, 0, pieces, tops, sums)


def partial_kernel(query_count, rows, *refs):
    query_refs, refs = refs[:query_count], refs[query_count:]
    key_refs, value_refs, outs, share = refs[:2], refs[2:4], refs[4:-1], refs[-1]
    columns = key_refs[0].shape[1]
    queries = jnp.concatenate([ref[:, :columns] for ref in query_refs], axis=0)
    for k, ref in enumerate(query_refs):
        share[k * rows : (k + 1) * rows, :] = ref[:, columns:]
    for found in weighed(queries, key_refs, value_refs, None, 0):
        store_packed(outs, rows, *found)


def merge_kernel(p, *refs):
    parts, weight, out = refs[:-2], refs[-2], refs[-1]
    shards, columns = len(parts), parts[0].shape[1]
    heads = columns // HEAD_DIM
    rows = out.shape[0]
    tops, sums = [], []
    for s in range(shards):
        top, total = joined_stats(parts[s][rows:, :].astype(f32)[:, :rows], heads)
        tops.append(top)
        sums.append(total)
    highest = functools.reduce(jnp.maximum, tops)
    factors = [jnp.exp(top - highest) for top in tops]
    total = sum(factor * one for factor, one in zip(factors, sums))
    factors = jnp.concatenate([factor / total for factor in factors], axis=0)
    shape = (shards * heads, shards * columns)
    row = lax.broadcasted_iota(jnp.int32, shape, 0)
    lane = lax.broadcasted_iota(jnp.int32, shape, 1)
    spreader = (lane // HEAD_DIM == row).astype(f32)
    factors = contracted(factors, spreader, 0, 0, lax.Precision.HIGHEST)
    context = jnp.zeros((rows, columns), f32)
    for s in range(shards):
        context += factors[:, s * columns : (s + 1) * columns] * parts[s][:rows, :].astype(f32)
    out[...] = product(context.astype(bf16), weight[p]).astype(bf16)


def updated(state, parts):
    terms = [part[...].astype(f32) for part in parts]
    while len(terms) > 1:
        terms = [first + second for first, second in zip(terms[0::2], terms[1::2])]
    return state[...] + terms[0]


def add_kernel(part, other, out):
    out[...] = (part[...].astype(f32) + other[...].astype(f32)).astype(bf16)


def project_kernel(p, scale, state, *refs):
    parts, (query_w, key_w, value_w, new_state, query, both) = refs[:-6], refs[-6:]
    value = updated(state, parts)
    new_state[...] = value
    value = normed(value)
    columns = query_w.shape[2]
    query[...] = (product(value, query_w[p]) * scale).astype(bf16)
    both[:, :columns] = product(value, key_w[p]).astype(bf16)
    both[:, columns:] = product(value, value_w[p]).astype(bf16)


def attend_kernel(p, query, *refs):
    blocks, weight, out = refs[:-2], refs[-2], refs[-1]
    rows, columns = query.shape
    heads = columns // HEAD_DIM
    lane_head = lax.broadcasted_iota(jnp.int32, (rows, columns), 1) // HEAD_DIM
    some = query[...]
    stacked = [jnp.where(lane_head == h, some, jnp.zeros_like(some)) for h in range(heads)]
    stacked = jnp.concatenate(stacked, axis=0)
    scores = [contracted(block[:, :columns], stacked, 1, 1) for block in blocks]
    top = functools.reduce(jnp.maximum, scores)
    top = jnp.max(top, axis=0, keepdims=True)
    terms = [jnp.exp(part - top) for part in scores]
    total = jnp.sum(sum(terms), axis=0, keepdims=True)
    share = jnp.concatenate([(part / total).astype(bf16) for part in terms], axis=0)
    values = jnp.concatenate([block[:, columns:] for block in blocks], axis=0)
    made = contracted(share, values, 0, 0)
    context = jnp.zeros((rows, columns), f32)
    for h in range(heads):
        context = jnp.where(lane_head == h, made[h * rows : (h + 1) * rows, :], context)
    out[...] = product(context.astype(bf16), weight[p]).astype(bf16)


def mlp_kernel(p, state, *refs):
    parts, (in_w, out_w, new_state, out) = refs[:-4], refs[-4:]
    value = updated(state, parts)
    new_state[...] = value
    hidden = product(normed(value), in_w[p])
    hidden = 0.5 * hidden * (1.0 + lax.erf(hidden * 0.5**0.5))
    out[...] = product(hidden.astype(bf16), out_w[p]).astype(bf16)


def query_kernel(p, scale, state, *refs):
    parts, (query_w, index, new_state, message) = refs[:-4], refs[-4:]
    value = updated(state, parts)
    new_state[...] = value
    columns = query_w.shape[2]
    message[:, :columns] = (product(normed(value), query_w[p]) * scale).astype(bf16)
    own = new_state[:, pl.ds(pl.multiple_of(index[0, 0] * columns, columns), columns)]
    message[:, columns:] = own.astype(bf16)


def final_kernel(count, state, *refs):
    parts, (share, other_share, me, new_state, midway) = refs[:-5], refs[-5:]
    new_state[...] = updated(state, parts)
    rows = new_state.shape[0]
    line, side = me[0, 0] // 2, lax.rem(me[0, 0], 2)
    for k in range(count // 2):
        place_of = 2 * origin(count // 2, WIDEST // 2, k, line)
        for block, at in ((share, place_of + side), (other_share, place_of + 1 - side)):
            start = pl.multiple_of(at * rows, rows)
            midway[pl.ds(start, rows), :] = block[k * rows : (k + 1) * rows, :].astype(f32)


def heads_parts(part):
    count = lax.axis_size("heads")

    def from_bits(value, bits):
        return lax.ppermute(value, "heads", [(i, i ^ bits) for i in range(count)])

    both = whole_call(add_kernel, shaped(part.shape, bf16), part, from_bits(part, 1))
    return [both] + [from_bits(both, bits) for bits in range(2, count, 2)]


def local(
    frames,
    latents,
    cross_query,
    cross_key,
    cross_value,
    cross_out,
    self_query,
    self_key,
    self_value,
    self_out,
    mlp_in,
    mlp_out,
):
    scale = 1.0 / HEAD_DIM**0.5
    passes, width, columns = cross_query.shape
    shards, me = lax.axis_size("frames"), lax.axis_index("frames")
    latent_count = latents.shape[0]
    rows = latent_count // shards
    stat_rows = -(-STATS * (columns // HEAD_DIM) // 16) * 16
    state_shape = shaped((rows, width), f32)
    part_shape = shaped((rows, width), bf16)
    row_shape = shaped((rows, columns), bf16)
    double_shape = shaped((rows, 2 * columns), bf16)
    packed_shape = shaped((rows + stat_rows, columns), bf16)
    state, queries, own, key_w, value_w = whole_call(
        functools.partial(latents_kernel, scale, shards),
        (
            state_shape,
            shaped((latent_count, columns), bf16),
            shaped(frames.shape, bf16),
            shaped((width, columns), bf16),
            shaped((width, columns), bf16),
        ),
        unplaced=(frames, cross_key, cross_value, latents, cross_query),
        scalars=(me,),
        scratch=[
            pltpu.VMEM((latent_count, width), bf16),
            pltpu.VMEM((width, columns), bf16),
            pltpu.VMEM((latent_count, width), bf16),
            pltpu.SemaphoreType.DMA((5,)),
        ],
        limit=LOAD_BYTES,
        cost=pl.CostEstimate(
            flops=2 * latent_count * width * columns,
            bytes_accessed=2 * latent_count * width,
            transcendentals=0,
        ),
    )
    frame_count = frames.shape[0]
    chunks = CHUNKS
    part_rows = frame_count // chunks
    count, side = lax.axis_size("heads"), lax.axis_index("heads")
    steps = range(2, count, 2)
    owners = [side, side ^ 1] + [(side - k) % count for k in steps]
    owners = owners + [((side ^ 1) - k) % count for k in steps]
    far = []
    for c in range(chunks):
        piece = lax.slice_in_dim(frames, c * part_rows, (c + 1) * part_rows, axis=0)
        far.append([shifted(piece, "heads", k) for k in steps])
    near = lax.ppermute(frames, "heads", [(i, i ^ 1) for i in range(count)])
    heads = columns // HEAD_DIM
    line_latents = latent_count // 2
    line_shape = shaped((columns + stat_rows, line_latents), bf16)
    results = [
        shaped((part_rows, width), bf16),
        shaped((part_rows, columns), bf16),
        shaped((columns, part_rows), bf16),
    ]

    def carry_of(latent_rows):
        return [shaped((columns, latent_rows), f32), shaped((2 * heads, latent_rows), f32)]

    pieces, carry = [], []
    for c in range(chunks):
        last = c + 1 == chunks
        served = line_latents if last else latent_count
        if c == 0:
            blocks, queries = pass_on(far[c], queries)
        else:
            blocks, pieces[-1] = pass_on(far[c], pieces[-1])
        made = whole_call(
            functools.partial(chunk_kernel, c, count, line_latents if last else 0, c > 0),
            results + [line_shape] if last else results[:1] + carry_of(latent_count),
            queries,
            key_w,
            value_w,
            own,
            near,
            *blocks,
            scalars=owners,
            after=carry,
            scratch=[] if last else [pltpu.VMEM(one.shape, one.dtype) for one in results[1:]],
            cost=pl.CostEstimate(
                flops=4 * part_rows * width * columns,
                bytes_accessed=2 * part_rows * width,
                transcendentals=heads * served * part_rows,
            ),
        )
        pieces.append(made[:1])
        if not last:
            carry = made[1:]
    other = pair_swap(made[3])
    carry = whole_call(
        own_kernel,
        carry_of(line_latents),
        queries,
        *made[1:3],
        *carry,
        cost=pl.CostEstimate(
            flops=4 * line_latents * part_rows * columns,
            bytes_accessed=4 * latent_count * columns,
            transcendentals=heads * line_latents * part_rows,
        ),
    )
    line_count = shards // 2
    first_parts = whole_call(
        functools.partial(fold_kernel, rows), [packed_shape] * line_count, *carry, other
    )
    key_values = [None] + [
        whole_call(
            functools.partial(key_value_kernel, p),
            (shaped((frame_count, columns), bf16), shaped((columns, frame_count), bf16)),
            *[piece[0] for piece in pieces],
            cross_key,
            cross_value,
            cost=pl.CostEstimate(
                flops=4 * frame_count * width * columns,
                bytes_accessed=2 * frame_count * width,
                transcendentals=0,
            ),
        )
        for p in range(1, passes)
    ]
    for p in range(passes):
        if p == 0:
            parts = line_return(first_parts)
        else:
            keys, values = key_values[p]
            results = [packed_shape] * len(queries) + [shaped((rows * len(queries), columns), bf16)]
            *parts, share = whole_call(
                functools.partial(partial_kernel, len(queries), rows),
                results,
                *queries,
                keys,
                pair_swap(keys),
                values,
                pair_swap(values),
            )
            parts = line_return(parts)
            if p == 1:
                first_share = share
        part = whole_call(functools.partial(merge_kernel, p), part_shape, *parts, cross_out)
        state, query, both = whole_call(
            functools.partial(project_kernel, p, scale),
            (state_shape, row_shape, double_shape),
            state,
            *heads_parts(part),
            self_query,
            self_key,
            self_value,
        )
        if shards > WIDEST:
            blocks = gathered_blocks(both, "frames")
        else:
            blocks = line_gather(both)
            blocks = blocks + [pair_swap(block) for block in blocks]
        part = whole_call(functools.partial(attend_kernel, p), part_shape, query, *blocks, self_out)
        state, part = whole_call(
            functools.partial(mlp_kernel, p),
            (state_shape, part_shape),
            state,
            *heads_parts(part),
            mlp_in,
            mlp_out,
        )
        parts = heads_parts(part)
        if p + 1 < passes:
            state, message = whole_call(
                functools.partial(query_kernel, p + 1, scale),
                (state_shape, double_shape),
                state,
                *parts,
                cross_query,
                scalars=(lax.axis_index("heads"),),
            )
            queries = line_gather(message)
        else:
            state, midway = whole_call(
                functools.partial(final_kernel, shards),
                (state_shape, shaped((latent_count, columns), f32)),
                state,
                *parts,
                first_share,
                pair_swap(first_share),
                scalars=(me,),
            )
    return (state, midway)


def solution(mesh):
    columns, rows = P(None, None, "heads"), P(None, "heads", None)
    placed = (P("frames", "heads"), P(), columns, columns, columns, rows)
    placed = placed + (columns, columns, columns, rows, columns, rows)
    return jax.shard_map(
        local,
        mesh=mesh,
        in_specs=placed,
        out_specs=(P("frames", None), P(None, "heads")),
        check_vma=False,
    )
```

```python
import functools

import jax
import jax.numpy as jnp
from jax import lax
from jax.experimental import pallas as pl
from jax.experimental.pallas import tpu as pltpu
from jax.sharding import PartitionSpec as P

HEAD_DIM = 64
STATS = 4
VMEM_BYTES = 10 << 20
LOAD_BYTES = 54 << 20
CHUNKS = 2
WIDEST = 8
epsilon = 1e-05
f32, bf16 = jnp.float32, jnp.bfloat16


def shifted(value, axis, step):
    count = lax.axis_size(axis)
    return lax.ppermute(value, axis, [(i, (i + step) % count) for i in range(count)])


def origin(count, widest, k, me):
    return k if count > widest else lax.rem(me - k + count, count)


def gathered_blocks(value, axis):
    count = lax.axis_size(axis)
    if count > WIDEST:
        pieces = lax.all_gather(value, axis)
        return [pieces[k] for k in range(count)]
    return [value] + [shifted(value, axis, k) for k in range(1, count)]


def line_of(count):
    return [list(range(x, count, 2)) for x in range(2)]


def line_shift(value, step):
    count = lax.axis_size("frames")
    return lax.ppermute(value, "frames", [(i, (i + 2 * step) % count) for i in range(count)])


def line_gather(value):
    count = lax.axis_size("frames")
    if count > WIDEST:
        pieces = lax.all_gather(value, "frames", axis_index_groups=line_of(count))
        return [pieces[k] for k in range(count // 2)]
    return [value] + [line_shift(value, k) for k in range(1, count // 2)]


def line_return(blocks):
    count = lax.axis_size("frames")
    if count > WIDEST:
        groups = line_of(count)
        pieces = lax.all_to_all(jnp.stack(blocks), "frames", 0, 0, axis_index_groups=groups)
        return [pieces[k] for k in range(count // 2)]
    return [blocks[0]] + [line_shift(blocks[k], -k) for k in range(1, count // 2)]


def pair_swap(value):
    count = lax.axis_size("frames")
    return lax.ppermute(value, "frames", [(i, i ^ 1) for i in range(count)])


def pass_on(blocks, alongside):
    count = lax.axis_size("heads")
    blocks, alongside = lax.optimization_barrier((blocks, alongside))
    swap = [(i, i ^ 1) for i in range(count)]
    return blocks + [lax.ppermute(block, "heads", swap) for block in blocks], alongside


def whole_call(body, results, *operands, cost=None, unplaced=(), scalars=(), after=(), scratch=(), limit=None):
    space = pl.BlockSpec(memory_space=pltpu.VMEM)
    specs = [pl.BlockSpec(memory_space=pltpu.HBM)] * len(unplaced) + [space] * len(operands)
    specs += [pl.BlockSpec(memory_space=pltpu.SMEM)] * len(scalars) + [space] * len(after)
    scalars = [jnp.asarray(index, jnp.int32).reshape(1, 1) for index in scalars]
    return pl.pallas_call(
        body,
        out_shape=results,
        in_specs=specs,
        out_specs=jax.tree.map(lambda _: space, results),
        scratch_shapes=scratch,
        compiler_params=pltpu.CompilerParams(vmem_limit_bytes=limit or VMEM_BYTES),
        cost_estimate=cost,
    )(*unplaced, *operands, *scalars, *after)


def shaped(shape, dtype):
    return jax.ShapeDtypeStruct(shape, dtype)


def normed(vector):
    centre = vector - jnp.mean(vector, axis=-1, keepdims=True)
    spread_sq = jnp.mean(centre * centre, axis=-1, keepdims=True)
    return (centre * lax.rsqrt(spread_sq + epsilon)).astype(bf16)


def product(left_side, weight):
    return jnp.dot(left_side, weight, preferred_element_type=f32)


def contracted(left_side, right_side, left_dim, right_dim, precision=None):
    return lax.dot_general(
        left_side,
        right_side,
        (((left_dim,), (right_dim,)), ((), ())),
        precision=precision,
        preferred_element_type=f32,
    )


def chunk_kernel(chunk, count, first_half, carried, last, *refs):
    queries, key_w, value_w = refs[:3]
    blocks, owners, refs = refs[3 : 3 + count], refs[3 + count : 3 + 2 * count], refs[3 + 2 * count :]
    carry, outs = (refs[:2], refs[2:]) if carried else (None, refs)
    out, keys, values = outs[:3]
    rows, width = out.shape[0], blocks[0].shape[1]
    served = queries.at[pl.ds(first_half, queries.shape[0] - first_half), :]
    tile = min(rows, 32)
    for start in range(0, rows, tile):
        pieces = []
        for block in blocks:
            first = start + (chunk * rows if block.shape[0] > rows else 0)
            pieces.append(block[first : first + tile, :].astype(f32))
        mean = jnp.sum(sum(pieces), axis=1, keepdims=True) / (width * count)
        pieces = [piece - mean for piece in pieces]
        total = jnp.sum(sum(piece * piece for piece in pieces), axis=1, keepdims=True)
        scale = lax.rsqrt(total / (width * count) + epsilon)
        for piece, owner in zip(pieces, owners):
            lanes = pl.ds(pl.multiple_of(owner[0, 0] * width, width), width)
            out[start : start + tile, lanes] = (piece * scale).astype(bf16)
    keys[...] = product(out[...], key_w[...]).astype(bf16)
    values[...] = product(out[...], value_w[...]).astype(bf16).T
    for found in weighed(served, [keys], [values], carry, 0):
        if last:
            store_terms(outs[3], *found)
        else:
            store_carry(outs[3], outs[4], *found)


def own_kernel(queries, keys, values, *refs):
    carry, (out, stats) = refs[:-2] or None, refs[-2:]
    served = queries.at[pl.ds(0, out.shape[1]), :]
    for found in weighed(served, [keys], [values], carry, 0):
        store_carry(out, stats, *found)


def key_value_kernel(p, *refs):
    row_refs, (key_w, value_w, keys, values) = refs[:-4], refs[-4:]
    start = 0
    for rows in row_refs:
        end = start + rows.shape[0]
        keys[start:end, :] = product(rows[...], key_w[p]).astype(bf16)
        values[:, start:end] = product(rows[...], value_w[p]).astype(bf16).T
        start = end


def latents_kernel(scale, count, frames_hbm, key_hbm, value_hbm, latents_hbm, query_hbm, me, *refs):
    state, queries, own, key_w, value_w, latents, query_w, rows_normed, sems = refs
    moves = [
        (latents_hbm, latents),
        (query_hbm.at[0], query_w),
        (frames_hbm, own),
        (key_hbm.at[0], key_w),
        (value_hbm.at[0], value_w),
    ]
    loads = [pltpu.make_async_copy(*move, sems.at[i]) for i, move in enumerate(moves)]
    for load in loads:
        load.start()
    rows = state.shape[0]
    line, side = me[0, 0] // 2, lax.rem(me[0, 0], 2)
    loads[0].wait()
    for j in range(count):
        k = j % (count // 2)
        index = 2 * origin(count // 2, WIDEST // 2, k, line) + (side if j == k else 1 - side)
        value = latents[pl.ds(pl.multiple_of(index * rows, rows), rows), :].astype(f32)
        rows_normed[j * rows : (j + 1) * rows, :] = normed(value)
    state[...] = latents[pl.ds(pl.multiple_of(me[0, 0] * rows, rows), rows), :].astype(f32)
    loads[1].wait()
    queries[...] = (product(rows_normed[...], query_w[...]) * scale).astype(bf16)
    for load in loads[2:]:
        load.wait()


def split_terms(value):
    high = value.astype(bf16).astype(f32)
    return high, (value - high).astype(bf16).astype(f32)


def weighed(queries, key_refs, value_refs, carry, carry_start):
    columns = key_refs[0].shape[1]
    latents = queries.shape[0]
    heads = columns // HEAD_DIM
    chunk = min(latents, 256)
    span = min(columns, 128)
    lane_head = lax.broadcasted_iota(jnp.int32, (chunk, span), 1) // HEAD_DIM

    def scores_of(start, h):
        lanes = slice(h * HEAD_DIM // span * span, (h * HEAD_DIM // span + 1) * span)
        some = queries[start : start + chunk, lanes]
        mine = lane_head == h % (span // HEAD_DIM)
        one = jnp.where(mine, some, jnp.zeros_like(some))
        return [contracted(keys[:, lanes], one, 1, 1) for keys in key_refs]

    order = [(start, h) for start in range(0, latents, chunk) for h in range(heads)]
    coming = scores_of(*order[0])
    for start in range(0, latents, chunk):
        pieces, tops, sums = [], [], []
        for h in range(heads):
            scores, following = coming, order.index((start, h)) + 1
            if following < len(order):
                coming = scores_of(*order[following])
            top = functools.reduce(
                jnp.maximum, [jnp.max(part, axis=0, keepdims=True) for part in scores]
            )
            own = slice(h * HEAD_DIM, (h + 1) * HEAD_DIM)
            place = slice(carry_start + start, carry_start + start + chunk)
            if carry is not None:
                before = carry[1][h : h + 1, place]
                top = jnp.maximum(top, before)
            high, low = split_terms(top)
            top = high + low
            terms = [jnp.exp(part - top) for part in scores]
            total = sum(jnp.sum(part, axis=0, keepdims=True) for part in terms)
            piece = sum(product(v[own, :], part.astype(bf16)) for v, part in zip(value_refs, terms))
            if carry is not None:
                factor = jnp.exp(before - top)
                total += factor * carry[1][heads + h : heads + h + 1, place]
                piece += factor * carry[0][own, place]
            pieces.append(piece)
            tops.append(top)
            sums.append(total)
        yield start, pieces, tops, sums


def store_carry(out, stats, start, pieces, tops, sums):
    for h, rows in enumerate(tops + sums):
        stats[h : h + 1, start : start + rows.shape[1]] = rows
    for h, piece in enumerate(pieces):
        out[h * HEAD_DIM : (h + 1) * HEAD_DIM, start : start + piece.shape[1]] = piece


def split_stats(tops, sums, count):
    tops, sums = [split_terms(top) for top in tops], [split_terms(total) for total in sums]
    rows = [pair[0] for pair in tops] + [pair[1] for pair in tops]
    rows += [pair[0] for pair in sums] + [pair[1] for pair in sums]
    rows += [jnp.zeros_like(rows[0])] * (count - len(rows))
    return jnp.concatenate(rows, axis=0)


def joined_stats(stats, heads):
    return stats[:heads] + stats[heads : 2 * heads], stats[2 * heads : 3 * heads] + stats[3 * heads : 4 * heads]


def store_terms(out, start, pieces, tops, sums):
    place = slice(start, start + pieces[0].shape[1])
    columns = len(pieces) * HEAD_DIM
    out[:columns, place] = jnp.concatenate(pieces, axis=0).astype(bf16)
    out[columns:, place] = split_stats(tops, sums, out.shape[0] - columns).astype(bf16)


def store_packed(outs, rows, start, pieces, tops, sums):
    columns = len(pieces) * HEAD_DIM
    turned = jnp.concatenate(pieces, axis=0).T.astype(bf16)
    stats = split_stats(tops, sums, outs[0].shape[0] - rows)
    for j in range(turned.shape[0] // rows):
        out = outs[start // rows + j]
        out[:rows, :] = turned[j * rows : (j + 1) * rows, :]
        piece = stats[:, j * rows : (j + 1) * rows]
        piece = jnp.concatenate([piece, jnp.zeros((piece.shape[0], columns - rows), f32)], axis=1)
        out[rows:, :] = piece.astype(bf16)


def fold_kernel(rows, carry_out, carry_stats, other, *outs):
    columns, _ = carry_out.shape
    heads = columns // HEAD_DIM
    tops, sums = carry_stats[:heads, :], carry_stats[heads:, :]
    other_tops, other_sums = joined_stats(other[columns:, :].astype(f32), heads)
    highest = jnp.maximum(tops, other_tops)
    factor, other_factor = jnp.exp(tops - highest), jnp.exp(other_tops - highest)
    total = factor * sums + other_factor * other_sums
    pieces = []
    for h in range(heads):
        own = slice(h * HEAD_DIM, (h + 1) * HEAD_DIM)
        piece = factor[h : h + 1] * carry_out[own, :]
        pieces.append(piece + other_factor[h : h + 1] * other[own, :].astype(f32))
    tops = [highest[h : h + 1] for h in range(heads)]
    sums = [total[h : h + 1] for h in range(heads)]
    store_packed(outs, rows, 0, pieces, tops, sums)


def partial_kernel(query_count, rows, *refs):
    query_refs, refs = refs[:query_count], refs[query_count:]
    key_refs, value_refs, outs, share = refs[:2], refs[2:4], refs[4:-1], refs[-1]
    columns = key_refs[0].shape[1]
    queries = jnp.concatenate([ref[:, :columns] for ref in query_refs], axis=0)
    for k, ref in enumerate(query_refs):
        share[k * rows : (k + 1) * rows, :] = ref[:, columns:]
    for found in weighed(queries, key_refs, value_refs, None, 0):
        store_packed(outs, rows, *found)


def merge_kernel(p, *refs):
    parts, weight, out = refs[:-2], refs[-2], refs[-1]
    shards, columns = len(parts), parts[0].shape[1]
    heads = columns // HEAD_DIM
    rows = out.shape[0]
    tops, sums = [], []
    for s in range(shards):
        top, total = joined_stats(parts[s][rows:, :].astype(f32)[:, :rows], heads)
        tops.append(top)
        sums.append(total)
    highest = functools.reduce(jnp.maximum, tops)
    factors = [jnp.exp(top - highest) for top in tops]
    total = sum(factor * one for factor, one in zip(factors, sums))
    factors = jnp.concatenate([factor / total for factor in factors], axis=0)
    shape = (shards * heads, shards * columns)
    row = lax.broadcasted_iota(jnp.int32, shape, 0)
    lane = lax.broadcasted_iota(jnp.int32, shape, 1)
    spreader = (lane // HEAD_DIM == row).astype(f32)
    factors = contracted(factors, spreader, 0, 0, lax.Precision.HIGHEST)
    context = jnp.zeros((rows, columns), f32)
    for s in range(shards):
        context += factors[:, s * columns : (s + 1) * columns] * parts[s][:rows, :].astype(f32)
    out[...] = product(context.astype(bf16), weight[p]).astype(bf16)


def updated(state, parts):
    terms = [part[...].astype(f32) for part in parts]
    while len(terms) > 1:
        terms = [first + second for first, second in zip(terms[0::2], terms[1::2])]
    return state[...] + terms[0]


def add_kernel(part, other, out):
    out[...] = (part[...].astype(f32) + other[...].astype(f32)).astype(bf16)


def project_kernel(p, scale, state, *refs):
    parts, (query_w, key_w, value_w, new_state, query, both) = refs[:-6], refs[-6:]
    value = updated(state, parts)
    new_state[...] = value
    value = normed(value)
    columns = query_w.shape[2]
    query[...] = (product(value, query_w[p]) * scale).astype(bf16)
    both[:, :columns] = product(value, key_w[p]).astype(bf16)
    both[:, columns:] = product(value, value_w[p]).astype(bf16)


def attend_kernel(p, query, *refs):
    blocks, weight, out = refs[:-2], refs[-2], refs[-1]
    rows, columns = query.shape
    heads = columns // HEAD_DIM
    lane_head = lax.broadcasted_iota(jnp.int32, (rows, columns), 1) // HEAD_DIM
    some = query[...]
    stacked = [jnp.where(lane_head == h, some, jnp.zeros_like(some)) for h in range(heads)]
    stacked = jnp.concatenate(stacked, axis=0)
    scores = [contracted(block[:, :columns], stacked, 1, 1) for block in blocks]
    top = functools.reduce(jnp.maximum, scores)
    top = jnp.max(top, axis=0, keepdims=True)
    terms = [jnp.exp(part - top) for part in scores]
    total = jnp.sum(sum(terms), axis=0, keepdims=True)
    share = jnp.concatenate([(part / total).astype(bf16) for part in terms], axis=0)
    values = jnp.concatenate([block[:, columns:] for block in blocks], axis=0)
    made = contracted(share, values, 0, 0)
    context = jnp.zeros((rows, columns), f32)
    for h in range(heads):
        context = jnp.where(lane_head == h, made[h * rows : (h + 1) * rows, :], context)
    out[...] = product(context.astype(bf16), weight[p]).astype(bf16)


def mlp_kernel(p, state, *refs):
    parts, (in_w, out_w, new_state, out) = refs[:-4], refs[-4:]
    value = updated(state, parts)
    new_state[...] = value
    hidden = product(normed(value), in_w[p])
    hidden = 0.5 * hidden * (1.0 + lax.erf(hidden * 0.5**0.5))
    out[...] = product(hidden.astype(bf16), out_w[p]).astype(bf16)


def query_kernel(p, scale, state, *refs):
    parts, (query_w, index, new_state, message) = refs[:-4], refs[-4:]
    value = updated(state, parts)
    new_state[...] = value
    columns = query_w.shape[2]
    message[:, :columns] = (product(normed(value), query_w[p]) * scale).astype(bf16)
    own = new_state[:, pl.ds(pl.multiple_of(index[0, 0] * columns, columns), columns)]
    message[:, columns:] = own.astype(bf16)


def final_kernel(count, state, *refs):
    parts, (share, other_share, me, new_state, midway) = refs[:-5], refs[-5:]
    new_state[...] = updated(state, parts)
    rows = new_state.shape[0]
    line, side = me[0, 0] // 2, lax.rem(me[0, 0], 2)
    for k in range(count // 2):
        place_of = 2 * origin(count // 2, WIDEST // 2, k, line)
        for block, at in ((share, place_of + side), (other_share, place_of + 1 - side)):
            start = pl.multiple_of(at * rows, rows)
            midway[pl.ds(start, rows), :] = block[k * rows : (k + 1) * rows, :].astype(f32)


def heads_parts(part):
    count = lax.axis_size("heads")

    def from_bits(value, bits):
        return lax.ppermute(value, "heads", [(i, i ^ bits) for i in range(count)])

    both = whole_call(add_kernel, shaped(part.shape, bf16), part, from_bits(part, 1))
    return [both] + [from_bits(both, bits) for bits in range(2, count, 2)]


def local(
    frames,
    latents,
    cross_query,
    cross_key,
    cross_value,
    cross_out,
    self_query,
    self_key,
    self_value,
    self_out,
    mlp_in,
    mlp_out,
):
    scale = 1.0 / HEAD_DIM**0.5
    passes, width, columns = cross_query.shape
    shards, me = lax.axis_size("frames"), lax.axis_index("frames")
    latent_count = latents.shape[0]
    rows = latent_count // shards
    stat_rows = -(-STATS * (columns // HEAD_DIM) // 16) * 16
    state_shape = shaped((rows, width), f32)
    part_shape = shaped((rows, width), bf16)
    row_shape = shaped((rows, columns), bf16)
    double_shape = shaped((rows, 2 * columns), bf16)
    packed_shape = shaped((rows + stat_rows, columns), bf16)
    state, queries, own, key_w, value_w = whole_call(
        functools.partial(latents_kernel, scale, shards),
        (
            state_shape,
            shaped((latent_count, columns), bf16),
            shaped(frames.shape, bf16),
            shaped((width, columns), bf16),
            shaped((width, columns), bf16),
        ),
        unplaced=(frames, cross_key, cross_value, latents, cross_query),
        scalars=(me,),
        scratch=[
            pltpu.VMEM((latent_count, width), bf16),
            pltpu.VMEM((width, columns), bf16),
            pltpu.VMEM((latent_count, width), bf16),
            pltpu.SemaphoreType.DMA((5,)),
        ],
        limit=LOAD_BYTES,
        cost=pl.CostEstimate(
            flops=2 * latent_count * width * columns,
            bytes_accessed=2 * latent_count * width,
            transcendentals=0,
        ),
    )
    frame_count = frames.shape[0]
    chunks = CHUNKS
    part_rows = frame_count // chunks
    count, side = lax.axis_size("heads"), lax.axis_index("heads")
    steps = range(2, count, 2)
    owners = [side, side ^ 1] + [(side - k) % count for k in steps]
    owners = owners + [((side ^ 1) - k) % count for k in steps]
    far = []
    for c in range(chunks):
        piece = lax.slice_in_dim(frames, c * part_rows, (c + 1) * part_rows, axis=0)
        far.append([shifted(piece, "heads", k) for k in steps])
    near = lax.ppermute(frames, "heads", [(i, i ^ 1) for i in range(count)])
    heads = columns // HEAD_DIM
    line_latents = latent_count // 2
    line_shape = shaped((columns + stat_rows, line_latents), bf16)
    results = [
        shaped((part_rows, width), bf16),
        shaped((part_rows, columns), bf16),
        shaped((columns, part_rows), bf16),
    ]

    carry_shapes = [
        shaped((columns, line_latents), f32),
        shaped((2 * heads, line_latents), f32),
    ]
    pieces, carry, own_carry = [], [], []
    for c in range(chunks):
        last = c + 1 == chunks
        if c == 0:
            blocks, queries = pass_on(far[c], queries)
        else:
            blocks, pieces[-1] = pass_on(far[c], pieces[-1])
        made = whole_call(
            functools.partial(chunk_kernel, c, count, line_latents, c > 0, last),
            results + ([line_shape] if last else carry_shapes),
            queries,
            key_w,
            value_w,
            own,
            near,
            *blocks,
            scalars=owners,
            after=carry,
            cost=pl.CostEstimate(
                flops=4 * part_rows * width * columns,
                bytes_accessed=2 * part_rows * width,
                transcendentals=heads * line_latents * part_rows,
            ),
        )
        pieces.append(made[:3])
        carry = made[3:]
        if last:
            other = pair_swap(made[3])
        own_carry = whole_call(
            own_kernel,
            carry_shapes,
            queries,
            *pieces[-1][1:3],
            *own_carry,
            cost=pl.CostEstimate(
                flops=4 * line_latents * part_rows * columns,
                bytes_accessed=4 * latent_count * columns,
                transcendentals=heads * line_latents * part_rows,
            ),
        )
    line_count = shards // 2
    first_parts = whole_call(
        functools.partial(fold_kernel, rows), [packed_shape] * line_count, *own_carry, other
    )
    key_values = [None] + [
        whole_call(
            functools.partial(key_value_kernel, p),
            (shaped((frame_count, columns), bf16), shaped((columns, frame_count), bf16)),
            *[piece[0] for piece in pieces],
            cross_key,
            cross_value,
            cost=pl.CostEstimate(
                flops=4 * frame_count * width * columns,
                bytes_accessed=2 * frame_count * width,
                transcendentals=0,
            ),
        )
        for p in range(1, passes)
    ]
    swapped = [None]
    for keys, values in key_values[1:]:
        keys = pair_swap(keys)
        swapped.append((keys, pair_swap(values)))
    for p in range(passes):
        if p == 0:
            parts = line_return(first_parts)
        else:
            keys, values = key_values[p]
            results = [packed_shape] * len(queries) + [shaped((rows * len(queries), columns), bf16)]
            *parts, share = whole_call(
                functools.partial(partial_kernel, len(queries), rows),
                results,
                *queries,
                keys,
                swapped[p][0],
                values,
                swapped[p][1],
            )
            parts = line_return(parts)
            if p == 1:
                shares = [share, pair_swap(share)]
        part = whole_call(functools.partial(merge_kernel, p), part_shape, *parts, cross_out)
        state, query, both = whole_call(
            functools.partial(project_kernel, p, scale),
            (state_shape, row_shape, double_shape),
            state,
            *heads_parts(part),
            self_query,
            self_key,
            self_value,
        )
        if shards > WIDEST:
            blocks = gathered_blocks(both, "frames")
        else:
            blocks = line_gather(both)
            blocks = blocks + [pair_swap(block) for block in blocks]
        part = whole_call(functools.partial(attend_kernel, p), part_shape, query, *blocks, self_out)
        parts = heads_parts(part)
        state, part = whole_call(
            functools.partial(mlp_kernel, p),
            (state_shape, part_shape),
            state,
            *parts,
            mlp_in,
            mlp_out,
        )
        parts = heads_parts(part)
        if p + 1 < passes:
            state, message = whole_call(
                functools.partial(query_kernel, p + 1, scale),
                (state_shape, double_shape),
                state,
                *parts,
                cross_query,
                scalars=(lax.axis_index("heads"),),
            )
            queries = line_gather(message)
        else:
            state, midway = whole_call(
                functools.partial(final_kernel, shards),
                (state_shape, shaped((latent_count, columns), f32)),
                state,
                *parts,
                *shares,
                scalars=(me,),
            )
    return (state, midway)


def solution(mesh):
    columns, rows = P(None, None, "heads"), P(None, "heads", None)
    placed = (P("frames", "heads"), P(), columns, columns, columns, rows)
    placed = placed + (columns, columns, columns, rows, columns, rows)
    return jax.shard_map(
        local,
        mesh=mesh,
        in_specs=placed,
        out_specs=(P("frames", None), P(None, "heads")),
        check_vma=False,
    )
```

```python
import functools

import jax
import jax.numpy as jnp
from jax import lax
from jax.experimental import pallas as pl
from jax.experimental.pallas import tpu as pltpu
from jax.sharding import PartitionSpec as P

HEAD_DIM = 64
STATS = 4
VMEM_BYTES = 10 << 20
LOAD_BYTES = 53 << 20
CHUNK_BYTES = 50 << 20
CHUNKS = 2
WIDEST = 8
epsilon = 1e-05
f32, bf16 = jnp.float32, jnp.bfloat16


def shifted(value, axis, step):
    count = lax.axis_size(axis)
    return lax.ppermute(value, axis, [(i, (i + step) % count) for i in range(count)])


def origin(count, widest, k, me):
    return k if count > widest else lax.rem(me - k + count, count)


def gathered_blocks(value, axis):
    count = lax.axis_size(axis)
    if count > WIDEST:
        pieces = lax.all_gather(value, axis)
        return [pieces[k] for k in range(count)]
    return [value] + [shifted(value, axis, k) for k in range(1, count)]


def line_of(count):
    return [list(range(x, count, 2)) for x in range(2)]


def line_shift(value, step):
    count = lax.axis_size("frames")
    return lax.ppermute(value, "frames", [(i, (i + 2 * step) % count) for i in range(count)])


def line_gather(value):
    count = lax.axis_size("frames")
    if count > WIDEST:
        pieces = lax.all_gather(value, "frames", axis_index_groups=line_of(count))
        return [pieces[k] for k in range(count // 2)]
    return [value] + [line_shift(value, k) for k in range(1, count // 2)]


def line_return(blocks):
    count = lax.axis_size("frames")
    if count > WIDEST:
        groups = line_of(count)
        pieces = lax.all_to_all(jnp.stack(blocks), "frames", 0, 0, axis_index_groups=groups)
        return [pieces[k] for k in range(count // 2)]
    return [blocks[0]] + [line_shift(blocks[k], -k) for k in range(1, count // 2)]


def pair_swap(value):
    count = lax.axis_size("frames")
    return lax.ppermute(value, "frames", [(i, i ^ 1) for i in range(count)])


def pass_on(blocks, alongside):
    count = lax.axis_size("heads")
    blocks, alongside = lax.optimization_barrier((blocks, alongside))
    swap = [(i, i ^ 1) for i in range(count)]
    return blocks + [lax.ppermute(block, "heads", swap) for block in blocks], alongside


def whole_call(body, results, *operands, cost=None, unplaced=(), scalars=(), after=(), scratch=(), limit=None):
    space = pl.BlockSpec(memory_space=pltpu.VMEM)
    specs = [pl.BlockSpec(memory_space=pltpu.HBM)] * len(unplaced) + [space] * len(operands)
    specs += [pl.BlockSpec(memory_space=pltpu.SMEM)] * len(scalars) + [space] * len(after)
    scalars = [jnp.asarray(index, jnp.int32).reshape(1, 1) for index in scalars]
    return pl.pallas_call(
        body,
        out_shape=results,
        in_specs=specs,
        out_specs=jax.tree.map(lambda _: space, results),
        scratch_shapes=scratch,
        compiler_params=pltpu.CompilerParams(vmem_limit_bytes=limit or VMEM_BYTES),
        cost_estimate=cost,
    )(*unplaced, *operands, *scalars, *after)


def shaped(shape, dtype):
    return jax.ShapeDtypeStruct(shape, dtype)


def normed(vector):
    centre = vector - jnp.mean(vector, axis=-1, keepdims=True)
    spread_sq = jnp.mean(centre * centre, axis=-1, keepdims=True)
    return (centre * lax.rsqrt(spread_sq + epsilon)).astype(bf16)


def product(left_side, weight):
    return jnp.dot(left_side, weight, preferred_element_type=f32)


def contracted(left_side, right_side, left_dim, right_dim, precision=None):
    return lax.dot_general(
        left_side,
        right_side,
        (((left_dim,), (right_dim,)), ((), ())),
        precision=precision,
        preferred_element_type=f32,
    )


def chunk_kernel(chunk, count, first_half, carried, last, *refs):
    frames_hbm, key_hbm, value_hbm, queries = refs[:4]
    blocks, owners, refs = refs[4 : 3 + count], refs[3 + count : 3 + 2 * count], refs[3 + 2 * count :]
    carry, refs = (refs[:2], refs[2:]) if carried else (None, refs)
    outs, (own, key_w, value_w, sems) = refs[:-4], refs[-4:]
    out, keys, values = outs[:3]
    rows, width = own.shape
    served = queries.at[pl.ds(first_half, queries.shape[0] - first_half), :]
    loads = [
        pltpu.make_async_copy(frames_hbm.at[pl.ds(chunk * rows, rows), :], own, sems.at[0]),
        pltpu.make_async_copy(key_hbm.at[0], key_w, sems.at[1]),
        pltpu.make_async_copy(value_hbm.at[0], value_w, sems.at[2]),
    ]
    for load in loads:
        load.start()
    loads[0].wait()
    blocks = [own] + list(blocks)
    tile = min(rows, 128)
    for start in range(0, rows, tile):
        pieces = []
        for block in blocks:
            first = start + (chunk * rows if block.shape[0] > rows else 0)
            pieces.append(block[first : first + tile, :].astype(f32))
        mean = jnp.sum(sum(pieces), axis=1, keepdims=True) / (width * count)
        pieces = [piece - mean for piece in pieces]
        total = jnp.sum(sum(piece * piece for piece in pieces), axis=1, keepdims=True)
        scale = lax.rsqrt(total / (width * count) + epsilon)
        for piece, owner in zip(pieces, owners):
            lanes = pl.ds(pl.multiple_of(owner[0, 0] * width, width), width)
            out[start : start + tile, lanes] = (piece * scale).astype(bf16)
    for load in loads[1:]:
        load.wait()
    keys[...] = product(out[...], key_w[...]).astype(bf16)
    values[...] = product(out[...], value_w[...]).astype(bf16).T
    for found in weighed(served, [keys], [values], carry, 0):
        if last:
            store_terms(outs[3], *found)
        else:
            store_carry(outs[3], outs[4], *found)


def own_kernel(queries, keys, values, *refs):
    carry, (out, stats) = refs[:-2] or None, refs[-2:]
    served = queries.at[pl.ds(0, out.shape[1]), :]
    for found in weighed(served, [keys], [values], carry, 0):
        store_carry(out, stats, *found)


def key_value_kernel(p, *refs):
    row_refs, (key_w, value_w, keys, values) = refs[:-4], refs[-4:]
    start = 0
    for rows in row_refs:
        end = start + rows.shape[0]
        keys[start:end, :] = product(rows[...], key_w[p]).astype(bf16)
        values[:, start:end] = product(rows[...], value_w[p]).astype(bf16).T
        start = end


def latents_kernel(scale, count, latents_hbm, query_hbm, me, *refs):
    state, queries, latents, query_w, rows_normed, sems = refs
    moves = [(latents_hbm, latents), (query_hbm.at[0], query_w)]
    loads = [pltpu.make_async_copy(*move, sems.at[i]) for i, move in enumerate(moves)]
    for load in loads:
        load.start()
    rows = state.shape[0]
    line, side = me[0, 0] // 2, lax.rem(me[0, 0], 2)
    loads[0].wait()
    for j in range(count):
        k = j % (count // 2)
        index = 2 * origin(count // 2, WIDEST // 2, k, line) + (side if j == k else 1 - side)
        value = latents[pl.ds(pl.multiple_of(index * rows, rows), rows), :].astype(f32)
        rows_normed[j * rows : (j + 1) * rows, :] = normed(value)
    state[...] = latents[pl.ds(pl.multiple_of(me[0, 0] * rows, rows), rows), :].astype(f32)
    loads[1].wait()
    queries[...] = (product(rows_normed[...], query_w[...]) * scale).astype(bf16)


def split_terms(value):
    high = value.astype(bf16).astype(f32)
    return high, (value - high).astype(bf16).astype(f32)


def weighed(queries, key_refs, value_refs, carry, carry_start):
    columns = key_refs[0].shape[1]
    latents = queries.shape[0]
    heads = columns // HEAD_DIM
    chunk = min(latents, 256)
    span = min(columns, 128)
    lane_head = lax.broadcasted_iota(jnp.int32, (chunk, span), 1) // HEAD_DIM

    def scores_of(start, h):
        lanes = slice(h * HEAD_DIM // span * span, (h * HEAD_DIM // span + 1) * span)
        some = queries[start : start + chunk, lanes]
        mine = lane_head == h % (span // HEAD_DIM)
        one = jnp.where(mine, some, jnp.zeros_like(some))
        return [contracted(keys[:, lanes], one, 1, 1) for keys in key_refs]

    order = [(start, h) for start in range(0, latents, chunk) for h in range(heads)]
    coming = scores_of(*order[0])
    for start in range(0, latents, chunk):
        pieces, tops, sums = [], [], []
        for h in range(heads):
            scores, following = coming, order.index((start, h)) + 1
            if following < len(order):
                coming = scores_of(*order[following])
            top = functools.reduce(
                jnp.maximum, [jnp.max(part, axis=0, keepdims=True) for part in scores]
            )
            own = slice(h * HEAD_DIM, (h + 1) * HEAD_DIM)
            place = slice(carry_start + start, carry_start + start + chunk)
            if carry is not None:
                before = carry[1][h : h + 1, place]
                top = jnp.maximum(top, before)
            high, low = split_terms(top)
            top = high + low
            terms = [jnp.exp(part - top) for part in scores]
            total = sum(jnp.sum(part, axis=0, keepdims=True) for part in terms)
            piece = sum(product(v[own, :], part.astype(bf16)) for v, part in zip(value_refs, terms))
            if carry is not None:
                factor = jnp.exp(before - top)
                total += factor * carry[1][heads + h : heads + h + 1, place]
                piece += factor * carry[0][own, place]
            pieces.append(piece)
            tops.append(top)
            sums.append(total)
        yield start, pieces, tops, sums


def store_carry(out, stats, start, pieces, tops, sums):
    for h, rows in enumerate(tops + sums):
        stats[h : h + 1, start : start + rows.shape[1]] = rows
    for h, piece in enumerate(pieces):
        out[h * HEAD_DIM : (h + 1) * HEAD_DIM, start : start + piece.shape[1]] = piece


def split_stats(tops, sums, count):
    tops, sums = [split_terms(top) for top in tops], [split_terms(total) for total in sums]
    rows = [pair[0] for pair in tops] + [pair[1] for pair in tops]
    rows += [pair[0] for pair in sums] + [pair[1] for pair in sums]
    rows += [jnp.zeros_like(rows[0])] * (count - len(rows))
    return jnp.concatenate(rows, axis=0)


def joined_stats(stats, heads):
    return stats[:heads] + stats[heads : 2 * heads], stats[2 * heads : 3 * heads] + stats[3 * heads : 4 * heads]


def store_terms(out, start, pieces, tops, sums):
    place = slice(start, start + pieces[0].shape[1])
    columns = len(pieces) * HEAD_DIM
    out[:columns, place] = jnp.concatenate(pieces, axis=0).astype(bf16)
    out[columns:, place] = split_stats(tops, sums, out.shape[0] - columns).astype(bf16)


def store_packed(outs, rows, start, pieces, tops, sums):
    columns = len(pieces) * HEAD_DIM
    turned = jnp.concatenate(pieces, axis=0).T.astype(bf16)
    stats = split_stats(tops, sums, outs[0].shape[0] - rows)
    for j in range(turned.shape[0] // rows):
        out = outs[start // rows + j]
        out[:rows, :] = turned[j * rows : (j + 1) * rows, :]
        piece = stats[:, j * rows : (j + 1) * rows]
        piece = jnp.concatenate([piece, jnp.zeros((piece.shape[0], columns - rows), f32)], axis=1)
        out[rows:, :] = piece.astype(bf16)


def fold_kernel(rows, carry_out, carry_stats, other, *outs):
    columns, _ = carry_out.shape
    heads = columns // HEAD_DIM
    tops, sums = carry_stats[:heads, :], carry_stats[heads:, :]
    other_tops, other_sums = joined_stats(other[columns:, :].astype(f32), heads)
    highest = jnp.maximum(tops, other_tops)
    factor, other_factor = jnp.exp(tops - highest), jnp.exp(other_tops - highest)
    total = factor * sums + other_factor * other_sums
    pieces = []
    for h in range(heads):
        own = slice(h * HEAD_DIM, (h + 1) * HEAD_DIM)
        piece = factor[h : h + 1] * carry_out[own, :]
        pieces.append(piece + other_factor[h : h + 1] * other[own, :].astype(f32))
    tops = [highest[h : h + 1] for h in range(heads)]
    sums = [total[h : h + 1] for h in range(heads)]
    store_packed(outs, rows, 0, pieces, tops, sums)


def partial_kernel(query_count, rows, *refs):
    query_refs, refs = refs[:query_count], refs[query_count:]
    key_refs, value_refs, outs, share = refs[:2], refs[2:4], refs[4:-1], refs[-1]
    columns = key_refs[0].shape[1]
    queries = jnp.concatenate([ref[:, :columns] for ref in query_refs], axis=0)
    for k, ref in enumerate(query_refs):
        share[k * rows : (k + 1) * rows, :] = ref[:, columns:]
    for found in weighed(queries, key_refs, value_refs, None, 0):
        store_packed(outs, rows, *found)


def merge_kernel(p, *refs):
    parts, weight, out = refs[:-2], refs[-2], refs[-1]
    shards, columns = len(parts), parts[0].shape[1]
    heads = columns // HEAD_DIM
    rows = out.shape[0]
    tops, sums = [], []
    for s in range(shards):
        top, total = joined_stats(parts[s][rows:, :].astype(f32)[:, :rows], heads)
        tops.append(top)
        sums.append(total)
    highest = functools.reduce(jnp.maximum, tops)
    factors = [jnp.exp(top - highest) for top in tops]
    total = sum(factor * one for factor, one in zip(factors, sums))
    factors = jnp.concatenate([factor / total for factor in factors], axis=0)
    shape = (shards * heads, shards * columns)
    row = lax.broadcasted_iota(jnp.int32, shape, 0)
    lane = lax.broadcasted_iota(jnp.int32, shape, 1)
    spreader = (lane // HEAD_DIM == row).astype(f32)
    factors = contracted(factors, spreader, 0, 0, lax.Precision.HIGHEST)
    context = jnp.zeros((rows, columns), f32)
    for s in range(shards):
        context += factors[:, s * columns : (s + 1) * columns] * parts[s][:rows, :].astype(f32)
    out[...] = product(context.astype(bf16), weight[p]).astype(bf16)


def updated(state, parts):
    terms = [part[...].astype(f32) for part in parts]
    while len(terms) > 1:
        terms = [first + second for first, second in zip(terms[0::2], terms[1::2])]
    return state[...] + terms[0]


def add_kernel(part, other, out):
    out[...] = (part[...].astype(f32) + other[...].astype(f32)).astype(bf16)


def project_kernel(p, scale, state, *refs):
    parts, (query_w, key_w, value_w, new_state, query, both) = refs[:-6], refs[-6:]
    value = updated(state, parts)
    new_state[...] = value
    value = normed(value)
    columns = query_w.shape[2]
    query[...] = (product(value, query_w[p]) * scale).astype(bf16)
    both[:, :columns] = product(value, key_w[p]).astype(bf16)
    both[:, columns:] = product(value, value_w[p]).astype(bf16)


def attend_kernel(p, query, *refs):
    blocks, weight, out = refs[:-2], refs[-2], refs[-1]
    rows, columns = query.shape
    heads = columns // HEAD_DIM
    lane_head = lax.broadcasted_iota(jnp.int32, (rows, columns), 1) // HEAD_DIM
    some = query[...]
    stacked = [jnp.where(lane_head == h, some, jnp.zeros_like(some)) for h in range(heads)]
    stacked = jnp.concatenate(stacked, axis=0)
    scores = [contracted(block[:, :columns], stacked, 1, 1) for block in blocks]
    top = functools.reduce(jnp.maximum, scores)
    top = jnp.max(top, axis=0, keepdims=True)
    terms = [jnp.exp(part - top) for part in scores]
    total = jnp.sum(sum(terms), axis=0, keepdims=True)
    share = jnp.concatenate([(part / total).astype(bf16) for part in terms], axis=0)
    values = jnp.concatenate([block[:, columns:] for block in blocks], axis=0)
    made = contracted(share, values, 0, 0)
    context = jnp.zeros((rows, columns), f32)
    for h in range(heads):
        context = jnp.where(lane_head == h, made[h * rows : (h + 1) * rows, :], context)
    out[...] = product(context.astype(bf16), weight[p]).astype(bf16)


def mlp_kernel(p, state, *refs):
    parts, (in_w, out_w, new_state, out) = refs[:-4], refs[-4:]
    value = updated(state, parts)
    new_state[...] = value
    hidden = product(normed(value), in_w[p])
    hidden = 0.5 * hidden * (1.0 + lax.erf(hidden * 0.5**0.5))
    out[...] = product(hidden.astype(bf16), out_w[p]).astype(bf16)


def query_kernel(p, scale, state, *refs):
    parts, (query_w, index, new_state, message) = refs[:-4], refs[-4:]
    value = updated(state, parts)
    new_state[...] = value
    columns = query_w.shape[2]
    message[:, :columns] = (product(normed(value), query_w[p]) * scale).astype(bf16)
    own = new_state[:, pl.ds(pl.multiple_of(index[0, 0] * columns, columns), columns)]
    message[:, columns:] = own.astype(bf16)


def final_kernel(count, state, *refs):
    parts, (share, other_share, me, new_state, midway) = refs[:-5], refs[-5:]
    new_state[...] = updated(state, parts)
    rows = new_state.shape[0]
    line, side = me[0, 0] // 2, lax.rem(me[0, 0], 2)
    for k in range(count // 2):
        place_of = 2 * origin(count // 2, WIDEST // 2, k, line)
        for block, at in ((share, place_of + side), (other_share, place_of + 1 - side)):
            start = pl.multiple_of(at * rows, rows)
            midway[pl.ds(start, rows), :] = block[k * rows : (k + 1) * rows, :].astype(f32)


def heads_parts(part):
    count = lax.axis_size("heads")

    def from_bits(value, bits):
        return lax.ppermute(value, "heads", [(i, i ^ bits) for i in range(count)])

    both = whole_call(add_kernel, shaped(part.shape, bf16), part, from_bits(part, 1))
    return [both] + [from_bits(both, bits) for bits in range(2, count, 2)]


def local(
    frames,
    latents,
    cross_query,
    cross_key,
    cross_value,
    cross_out,
    self_query,
    self_key,
    self_value,
    self_out,
    mlp_in,
    mlp_out,
):
    scale = 1.0 / HEAD_DIM**0.5
    passes, width, columns = cross_query.shape
    shards, me = lax.axis_size("frames"), lax.axis_index("frames")
    latent_count = latents.shape[0]
    rows = latent_count // shards
    stat_rows = -(-STATS * (columns // HEAD_DIM) // 16) * 16
    state_shape = shaped((rows, width), f32)
    part_shape = shaped((rows, width), bf16)
    row_shape = shaped((rows, columns), bf16)
    double_shape = shaped((rows, 2 * columns), bf16)
    packed_shape = shaped((rows + stat_rows, columns), bf16)
    state, queries = whole_call(
        functools.partial(latents_kernel, scale, shards),
        (
            state_shape,
            shaped((latent_count, columns), bf16),
        ),
        unplaced=(latents, cross_query),
        scalars=(me,),
        scratch=[
            pltpu.VMEM((latent_count, width), bf16),
            pltpu.VMEM((width, columns), bf16),
            pltpu.VMEM((latent_count, width), bf16),
            pltpu.SemaphoreType.DMA((2,)),
        ],
        limit=LOAD_BYTES,
        cost=pl.CostEstimate(
            flops=2 * latent_count * width * columns,
            bytes_accessed=2 * latent_count * width,
            transcendentals=0,
        ),
    )
    frame_count = frames.shape[0]
    chunks = CHUNKS
    part_rows = frame_count // chunks
    count, side = lax.axis_size("heads"), lax.axis_index("heads")
    steps = range(2, count, 2)
    owners = [side, side ^ 1] + [(side - k) % count for k in steps]
    owners = owners + [((side ^ 1) - k) % count for k in steps]
    far = []
    for c in range(chunks):
        piece = lax.slice_in_dim(frames, c * part_rows, (c + 1) * part_rows, axis=0)
        far.append([shifted(piece, "heads", k) for k in steps])
    near = lax.ppermute(frames, "heads", [(i, i ^ 1) for i in range(count)])
    heads = columns // HEAD_DIM
    line_latents = latent_count // 2
    line_shape = shaped((columns + stat_rows, line_latents), bf16)
    results = [
        shaped((part_rows, width), bf16),
        shaped((part_rows, columns), bf16),
        shaped((columns, part_rows), bf16),
    ]

    carry_shapes = [
        shaped((columns, line_latents), f32),
        shaped((2 * heads, line_latents), f32),
    ]
    pieces, carry, own_carry = [], [], []
    for c in range(chunks):
        last = c + 1 == chunks
        if c == 0:
            blocks, queries = pass_on(far[c], queries)
        else:
            blocks, pieces[-1] = pass_on(far[c], pieces[-1])
        made = whole_call(
            functools.partial(chunk_kernel, c, count, line_latents, c > 0, last),
            results + ([line_shape] if last else carry_shapes),
            queries,
            near,
            *blocks,
            unplaced=(frames, cross_key, cross_value),
            scalars=owners,
            after=carry,
            limit=CHUNK_BYTES,
            scratch=[
                pltpu.VMEM((part_rows, frames.shape[1]), bf16),
                pltpu.VMEM((width, columns), bf16),
                pltpu.VMEM((width, columns), bf16),
                pltpu.SemaphoreType.DMA((3,)),
            ],
            cost=pl.CostEstimate(
                flops=4 * part_rows * width * columns,
                bytes_accessed=2 * part_rows * width,
                transcendentals=heads * line_latents * part_rows,
            ),
        )
        pieces.append(made[:3])
        carry = made[3:]
        if last:
            other = pair_swap(made[3])
        own_carry = whole_call(
            own_kernel,
            carry_shapes,
            queries,
            *pieces[-1][1:3],
            *own_carry,
            cost=pl.CostEstimate(
                flops=4 * line_latents * part_rows * columns,
                bytes_accessed=4 * latent_count * columns,
                transcendentals=heads * line_latents * part_rows,
            ),
        )
    line_count = shards // 2
    first_parts = whole_call(
        functools.partial(fold_kernel, rows), [packed_shape] * line_count, *own_carry, other
    )
    key_values = [None] + [
        whole_call(
            functools.partial(key_value_kernel, p),
            (shaped((frame_count, columns), bf16), shaped((columns, frame_count), bf16)),
            *[piece[0] for piece in pieces],
            cross_key,
            cross_value,
            cost=pl.CostEstimate(
                flops=4 * frame_count * width * columns,
                bytes_accessed=2 * frame_count * width,
                transcendentals=0,
            ),
        )
        for p in range(1, passes)
    ]
    swapped = [None]
    for keys, values in key_values[1:]:
        keys = pair_swap(keys)
        swapped.append((keys, pair_swap(values)))
    for p in range(passes):
        if p == 0:
            parts = line_return(first_parts)
        else:
            keys, values = key_values[p]
            results = [packed_shape] * len(queries) + [shaped((rows * len(queries), columns), bf16)]
            *parts, share = whole_call(
                functools.partial(partial_kernel, len(queries), rows),
                results,
                *queries,
                keys,
                swapped[p][0],
                values,
                swapped[p][1],
            )
            parts = line_return(parts)
            if p == 1:
                shares = [share, pair_swap(share)]
        part = whole_call(functools.partial(merge_kernel, p), part_shape, *parts, cross_out)
        state, query, both = whole_call(
            functools.partial(project_kernel, p, scale),
            (state_shape, row_shape, double_shape),
            state,
            *heads_parts(part),
            self_query,
            self_key,
            self_value,
        )
        if shards > WIDEST:
            blocks = gathered_blocks(both, "frames")
        else:
            blocks = line_gather(both)
            blocks = blocks + [pair_swap(block) for block in blocks]
        part = whole_call(functools.partial(attend_kernel, p), part_shape, query, *blocks, self_out)
        parts = heads_parts(part)
        state, part = whole_call(
            functools.partial(mlp_kernel, p),
            (state_shape, part_shape),
            state,
            *parts,
            mlp_in,
            mlp_out,
        )
        parts = heads_parts(part)
        if p + 1 < passes:
            state, message = whole_call(
                functools.partial(query_kernel, p + 1, scale),
                (state_shape, double_shape),
                state,
                *parts,
                cross_query,
                scalars=(lax.axis_index("heads"),),
            )
            queries = line_gather(message)
        else:
            state, midway = whole_call(
                functools.partial(final_kernel, shards),
                (state_shape, shaped((latent_count, columns), f32)),
                state,
                *parts,
                *shares,
                scalars=(me,),
            )
    return (state, midway)


def solution(mesh):
    columns, rows = P(None, None, "heads"), P(None, "heads", None)
    placed = (P("frames", "heads"), P(), columns, columns, columns, rows)
    placed = placed + (columns, columns, columns, rows, columns, rows)
    return jax.shard_map(
        local,
        mesh=mesh,
        in_specs=placed,
        out_specs=(P("frames", None), P(None, "heads")),
        check_vma=False,
    )
```
